128 devices in a mesh: req: 8 (over y, core), exp: 16 (over x, z).
Axes of the slice: x: 4, y: 4, z: 4, core: 2. Of those that a mesh axis runs over, the one named last changes fastest.
Arguments:
- tokens: bfloat16 [49152, 1536], P(('req', 'exp')), may hold values from -30 to 30
- segment_lengths: int32 [8, 16], P('req'), may hold values from 1 to 3071, as said below
- segment_adapters: int32 [8, 16], P('req'), may hold values from 0 to 15
- routes: int32 [49152, 4], P(('req', 'exp')), may hold values from 0 to 31, all different within a row; in each aligned block of 384 rows (0 to 383, 384 to 767, ...) at most 64 rows name the same one
- gate_weights: float32 [49152, 4], P(('req', 'exp')), may hold values from 0.05 to 1
- attention_gain: float32 [1536], replicated, may hold values from 0.5 to 1.5
- attention_in: bfloat16 [1536, 2048], P(None, 'req'), may hold values from -5 to 5
- sink_logits: float32 [12], replicated, may hold values from 0 to 6
- attention_out: bfloat16 [1536, 1536], P(None, 'req'), may hold values from -0.15625 to 0.15625
- expert_gain: float32 [1536], replicated, may hold values from 0.5 to 1.5
- expert_gate_up: bfloat16 [32, 1536, 1536], P('exp'), may hold values from -0.15625 to 0.15625
- expert_down: bfloat16 [32, 768, 1536], P('exp'), may hold values from -0.21875 to 0.21875
- adapter_in_down: bfloat16 [16, 1536, 16], P('req'), may hold values from -0.15625 to 0.15625
- adapter_in_up: bfloat16 [16, 16, 2048], P('req'), may hold values from -0.625 to 0.625
- adapter_out_down: bfloat16 [16, 1536, 16], P('req'), may hold values from -0.15625 to 0.15625
- adapter_out_up: bfloat16 [16, 16, 1536], P('req'), may hold values from -0.625 to 0.625
- adapter_expert_down: bfloat16 [16, 1536, 16], P('req'), may hold values from -0.15625 to 0.15625
- adapter_expert_up: bfloat16 [16, 32, 16, 768], P('req', 'exp'), may hold values from -0.625 to 0.625
Outputs:
- layer_output: bfloat16 [49152, 1536], P(('req', 'exp'))
The draws below stay inside these ranges and needn't reach their ends.
Inputs may be any that keep to these rules, and one draw needn't show every extreme that they name: `segment_lengths`: each row sums to 6144; entry 0 is the group's shared prompt of 1536 to 3071 tokens, the other entries are its requests, none longer than the prompt's most. `routes`: in each aligned block of 384 token rows (the rows of one device) no expert is named more than 64 times, a bound that some block reaches; a row names 4 different experts.
All inputs are finite; a program needn't handle non-finite values.
Results may differ from the reference program's by a relative error of at most 0.012.
The reference program's roundings to bfloat16 on the way count: a program that leaves them out, or rounds other values in their place, can miss the bound.
Values may be sent and summed in bfloat16 or wider, within the bound.
A program may use at most 128 MiB of HBM per device.

```python
import math
import jax
import jax.numpy as jnp
import numpy as np
from jax import lax

D = 1536
HEADS = 12
KVH = 2
HD = 128
EXPERTS = 32
FFE = 768
TOPK = 4
RANK = 16
WINDOW = 4096
SEGS = 16
TOK_DEV = 384
CAP = 64
QKVW = 2048
SPAN = 6144
GROUPS = 8
TOKENS = 49152
ADAPTERS = 16
N_EXP = 16


def draw_tokens(key, part):
    base_key = jax.random.fold_in(key, 0)
    values = jax.random.normal(base_key, (TOKENS, D), jnp.float32)
    return jnp.clip(values, -30.0, 30.0).astype(jnp.bfloat16)


def draw_attention_in(key, part):
    values = jax.random.normal(key, (D, QKVW), jnp.float32) * D ** (-0.5)
    return jnp.clip(values, -5.0, 5.0).astype(jnp.bfloat16)


def draw_segment_lengths(key, part):
    prompt_key, share_key = jax.random.split(key)
    prompt = SPAN // 4 + jax.random.randint(prompt_key, (GROUPS, 1), 0, SPAN // 4)
    prompt = prompt.at[0, 0].set(SPAN // 2 - 1)
    shares = jax.random.randint(share_key, (GROUPS, SEGS - 1), 1, 9)
    remaining = SPAN - prompt
    pieces = remaining * shares // jnp.sum(shares, axis=1, keepdims=True)
    pieces = pieces.at[:, -1].add(remaining[:, 0] - jnp.sum(pieces, axis=1))
    pieces = pieces.at[0, -2].add(pieces[0, -1] - 1)
    pieces = pieces.at[0, -1].set(1)
    return jnp.concatenate([prompt, pieces], axis=1).astype(jnp.int32)


def set_ends(drawn, stream_key, least, top_value):
    longest = drawn.shape.index(max(drawn.shape))
    spots = []
    for shift in (0, 1):
        where = [jax.random.randint(jax.random.fold_in(stream_key, axis), (), 0, length) for axis, length in enumerate(drawn.shape)]
        where[longest] = (where[longest] + shift) % drawn.shape[longest]
        spots.append(tuple(where))
    return drawn.at[spots[0]].set(least).at[spots[1]].set(top_value)


def shard_levels(rng, dims, shards, low, largest):
    factor_of = 1.0
    for position, blocks in shards:
        heights = jax.random.uniform(jax.random.fold_in(jax.random.fold_in(rng, 6), position), (blocks,), jnp.float32, low / len(shards), largest / len(shards))
        factor_of = factor_of * jnp.repeat(jnp.exp(heights), dims[position] // blocks).reshape((-1,) + (1,) * (len(dims) - 1 - position))
    return factor_of


def routed_block(own_key, own, number, rows, count, top, limit, skew):
    sequence = jax.random.permutation(own_key, count)
    heavy_load, common = portions_of(count, rows * top, limit, skew, True), portions_of(count, rows * top, limit, skew, False)
    places = jnp.arange(count)

    def named(sizes, rotation):
        used = int((sizes > 0).sum())
        fixed = max(1, used // 4)
        passed = fixed + (places - fixed + rotation * (used - fixed)) % max(1, count - fixed)
        return jnp.zeros((count,), jnp.int32).at[sequence[jnp.where(places < fixed, places, passed)]].set(jnp.asarray(sizes, jnp.int32))

    sizes = jnp.where(number % 4 == 0, named(heavy_load, number // 4), named(common, number - number // 4 - 1))
    mixed = jax.random.permutation(jax.random.fold_in(own, 3), count)
    giver, receiver = mixed[0:count // 2 * 2:2], mixed[1:count // 2 * 2:2]
    margin = jnp.minimum(sizes[giver] - 1, limit - sizes[receiver]) // 2
    margin = jnp.where((giver == sequence[0]) | (receiver == sequence[0]) | (sizes[receiver] == 0), 0, jnp.maximum(margin, 0))
    passed = jax.random.randint(jax.random.fold_in(own, 4), (count // 2,), 0, 1 << 20) % (margin + 1)
    sizes = sizes.at[giver].add(-passed).at[receiver].add(passed)
    members = jnp.searchsorted(jnp.cumsum(sizes), jnp.arange(rows * top), side="right").astype(jnp.int32)
    table = members.reshape(top, rows).T
    table = table[jax.random.permutation(jax.random.fold_in(own, 1), rows)]
    rotation = jax.random.randint(jax.random.fold_in(own, 2), (rows, 1), 0, top)
    return jnp.take_along_axis(table, (jnp.arange(top)[None, :] + rotation) % top, axis=1)


def portions_of(number_of, total, limit, slope, full):
    loads = [(1 << 20) // math.isqrt(standing ** slope) + 1 for standing in range(1, number_of + 1)]
    largest = limit if full else min(limit, max(-(-total // number_of), total * loads[0] // sum(loads)))
    least = 1 if total - largest >= number_of - 1 else 0
    counts, surplus = [largest] + [least] * (number_of - 1), total - largest - least * (number_of - 1)
    while surplus > 0:
        movable = [i for i in range(1, number_of) if counts[i] < largest] or [i for i in range(1, number_of) if counts[i] < limit]
        mass, left = sum([loads[i] for i in movable]), surplus
        for i in movable:
            addition = min(limit - counts[i], max(1, left * loads[i] // mass), surplus)
            counts[i] = counts[i] + addition
            surplus = surplus - addition
    return np.array(counts)


def scatter_about(stream_key, extent, width, most, cuts=(), kind=jnp.bfloat16):
    result = jax.random.normal(stream_key, extent, jnp.float32) * width
    if len(cuts) > 0:
        result = shard_levels(stream_key, extent, cuts, -0.22, 0.18) * result
    return jnp.clip(result, min=-most, max=most).astype(kind)


def setup_inputs(seed: int = 0) -> dict:
    seeds = jax.random.split(jax.random.key(seed), 19)
    tokens = draw_tokens(jax.random.fold_in(seeds[18], 71), 0)
    segment_lengths = draw_segment_lengths(jax.random.fold_in(seeds[18], 71), 0)
    segment_adapters = set_ends(jax.random.randint(seeds[2], (GROUPS, SEGS), 0, ADAPTERS), jax.random.fold_in(seeds[2], 1), 0, ADAPTERS - 1).astype(jnp.int32)
    routes_keys = jax.random.split(jax.random.fold_in(seeds[3], 1), TOKENS // TOK_DEV)
    routes_turns = jax.random.permutation(jax.random.fold_in(seeds[3], 3), TOKENS // TOK_DEV)
    routes = jax.vmap(lambda own, number: routed_block(jax.random.fold_in(seeds[3], 2), own, number, TOK_DEV, EXPERTS, TOPK, CAP, 2))(routes_keys, routes_turns).reshape((TOKENS, TOPK))
    gate_weights = jnp.clip(jnp.exp(math.log(1.0) - 2.9957323 * jax.random.uniform(seeds[4], (TOKENS, TOPK), jnp.float32) ** shard_levels(seeds[4], (TOKENS, TOPK), ((0, 128),), -0.2, 0.2)), 0.05, 1.0)
    attention_gain = jnp.clip(1.0 + 0.1 * jax.random.normal(seeds[5], (D,), jnp.float32), 0.5, 1.5)
    attention_in = draw_attention_in(jax.random.fold_in(seeds[18], 71), 0)
    sink_logits = jnp.clip(jax.random.uniform(seeds[7], (HEADS,), jnp.float32, 0.0, 6.0), 0.0, 6.0)
    attention_out = scatter_about(seeds[8], (HEADS * HD, D), (HEADS * HD) ** -0.5, 0.15625, ((1, 8),))
    expert_gain = jnp.clip(1.0 + 0.1 * jax.random.normal(seeds[9], (D,), jnp.float32), 0.5, 1.5)
    expert_gate_up = scatter_about(seeds[10], (EXPERTS, D, 2 * FFE), D ** -0.5, 0.15625, ((0, 16),))
    expert_down = scatter_about(seeds[11], (EXPERTS, FFE, D), FFE ** -0.5, 0.21875, ((0, 16),))
    adapter_in_down = scatter_about(seeds[12], (ADAPTERS, D, RANK), D ** -0.5, 0.15625, ((0, 8),))
    adapter_in_up = scatter_about(seeds[13], (ADAPTERS, RANK, QKVW), 0.1, 0.625, ((0, 8),))
    adapter_out_down = scatter_about(seeds[14], (ADAPTERS, HEADS * HD, RANK), (HEADS * HD) ** -0.5, 0.15625, ((0, 8),))
    adapter_out_up = scatter_about(seeds[15], (ADAPTERS, RANK, D), 0.1, 0.625, ((0, 8),))
    adapter_expert_down = scatter_about(seeds[16], (ADAPTERS, D, RANK), D ** -0.5, 0.15625, ((0, 8),))
    adapter_expert_up = scatter_about(seeds[17], (ADAPTERS, EXPERTS, RANK, FFE), 0.1, 0.625, ((0, 8), (1, 16)))
    return dict(tokens=tokens, segment_lengths=segment_lengths, segment_adapters=segment_adapters, routes=routes, gate_weights=gate_weights, attention_gain=attention_gain, attention_in=attention_in, sink_logits=sink_logits, attention_out=attention_out, expert_gain=expert_gain, expert_gate_up=expert_gate_up, expert_down=expert_down, adapter_in_down=adapter_in_down, adapter_in_up=adapter_in_up, adapter_out_down=adapter_out_down, adapter_out_up=adapter_out_up, adapter_expert_down=adapter_expert_down, adapter_expert_up=adapter_expert_up)


EPSILON = 1e-06
NEGATIVE = -1e+30

def scaled_norm(inputs, gain):
    floats = inputs.astype(jnp.float32)
    inverse = lax.rsqrt(lax.optimization_barrier(jnp.mean(floats * floats, axis=-1, keepdims=True)) + EPSILON)
    return (floats * inverse * gain).astype(jnp.bfloat16)

def segment_of(positions, lengths):
    seg_ends = jnp.cumsum(lengths)
    return lax.optimization_barrier(jnp.sum((positions[:, None] >= seg_ends[None, :]).astype(jnp.int32), axis=1))

def adapter_select(token_adapter, adapter_count, rank_size):
    owners = jnp.repeat(jnp.arange(adapter_count, dtype=jnp.int32), rank_size)
    return token_adapter[:, None] == owners[None, :]

def low_coords(inputs, select, first_factor):
    adapter_count, inner_width, rank_size = first_factor.shape
    joined = jnp.transpose(first_factor, (1, 0, 2)).reshape(inner_width, adapter_count * rank_size)
    coords = jnp.dot(inputs, joined, preferred_element_type=jnp.float32)
    return jnp.where(select, coords, 0.0).astype(jnp.bfloat16)

def low_rank(inputs, select, first_factor, second_factor):
    coords = low_coords(inputs, select, first_factor)
    adapter_count, rank_size, outer_width = second_factor.shape
    return jnp.dot(coords, second_factor.reshape(adapter_count * rank_size, outer_width), preferred_element_type=jnp.float32)

def reference(tokens, segment_lengths, segment_adapters, routes, gate_weights, attention_gain, attention_in, sink_logits, attention_out, expert_gain, expert_gate_up, expert_down, adapter_in_down, adapter_in_up, adapter_out_down, adapter_out_up, adapter_expert_down, adapter_expert_up):
    positions = jnp.arange(SPAN, dtype=jnp.int32)
    segments = jax.vmap(lambda lengths: segment_of(positions, lengths))(segment_lengths)
    token_adapter = jnp.take_along_axis(segment_adapters, segments, axis=1).reshape(TOKENS)
    select = adapter_select(token_adapter, ADAPTERS, RANK)
    normed = scaled_norm(tokens, attention_gain)
    projected = (jnp.dot(normed, attention_in, preferred_element_type=jnp.float32) + low_rank(normed, select, adapter_in_down, adapter_in_up)).astype(jnp.bfloat16)
    projected = lax.optimization_barrier(projected)
    group_size = HEADS // KVH
    sink_grid = sink_logits.reshape(KVH, group_size)[None]
    reach = min(SPAN, WINDOW + TOK_DEV)

    def attend_tile(tile_index):
        group_index = tile_index // N_EXP
        first_pos = (tile_index * TOK_DEV - group_index * SPAN).astype(jnp.int32)
        key_start = jnp.clip(first_pos + TOK_DEV - reach, 0, SPAN - reach).astype(jnp.int32)
        tile_rows = lax.dynamic_slice_in_dim(projected, tile_index * TOK_DEV, TOK_DEV, 0)
        block_rows = lax.dynamic_slice_in_dim(projected, group_index * SPAN + key_start, reach, 0)
        queries = tile_rows[:, :HEADS * HD].astype(jnp.float32).reshape(TOK_DEV, KVH, group_size, HD)
        key_part = block_rows[:, HEADS * HD:HEADS * HD + KVH * HD].astype(jnp.float32).reshape(reach, KVH, HD)
        value_part = block_rows[:, HEADS * HD + KVH * HD:].astype(jnp.float32).reshape(reach, KVH, HD)
        lengths = lax.dynamic_index_in_dim(segment_lengths, group_index, 0, keepdims=False)
        query_pos = first_pos + jnp.arange(TOK_DEV, dtype=jnp.int32)
        key_pos = key_start + jnp.arange(reach, dtype=jnp.int32)
        query_seg = segment_of(query_pos, lengths)
        key_seg = segment_of(key_pos, lengths)
        allowed = (key_pos[None, :] <= query_pos[:, None]) & (query_pos[:, None] - key_pos[None, :] < WINDOW)
        allowed = allowed & ((key_seg[None, :] == query_seg[:, None]) | (key_seg[None, :] == 0))
        scores = jnp.einsum('tkgd,skd->tkgs', queries, key_part) * HD ** (-0.5)
        scores = jnp.where(allowed[:, None, None, :], scores, NEGATIVE)
        running_max = jnp.maximum(lax.optimization_barrier(jnp.max(scores, axis=-1)), sink_grid)
        weights = jnp.exp(scores - running_max[..., None])
        denominator = lax.optimization_barrier(jnp.sum(weights, axis=-1)) + jnp.exp(sink_grid - running_max)
        rounded = lax.optimization_barrier(weights.astype(jnp.bfloat16)).astype(jnp.float32)
        mixed = jnp.einsum('tkgs,skd->tkgd', rounded, value_part) / denominator[..., None]
        return mixed.reshape(TOK_DEV, HEADS * HD).astype(jnp.bfloat16)
    attended = lax.map(attend_tile, jnp.arange(TOKENS // TOK_DEV, dtype=jnp.int32)).reshape(TOKENS, HEADS * HD)
    attended = lax.optimization_barrier(attended)
    residual = (tokens.astype(jnp.float32) + jnp.dot(attended, attention_out, preferred_element_type=jnp.float32) + low_rank(attended, select, adapter_out_down, adapter_out_up)).astype(jnp.bfloat16)
    residual = lax.optimization_barrier(residual)
    normed_two = scaled_norm(residual, expert_gain)
    expert_coords = low_coords(normed_two, select, adapter_expert_down)
    block_count = TOKENS // TOK_DEV
    picked = routes.reshape(block_count, TOK_DEV * TOPK)
    expert_hot = (picked[:, :, None] == jnp.arange(EXPERTS, dtype=jnp.int32)[None, None, :]).astype(jnp.int32)
    arrival = lax.optimization_barrier(jnp.sum((jnp.cumsum(expert_hot, axis=1) - 1) * expert_hot, axis=2))
    slot_index = picked * CAP + arrival
    pick_ids = jnp.broadcast_to(jnp.arange(TOK_DEV * TOPK, dtype=jnp.int32)[None, :], slot_index.shape)
    block_ids = jnp.broadcast_to(jnp.arange(block_count, dtype=jnp.int32)[:, None], slot_index.shape)
    slot_table = jnp.full((block_count, EXPERTS * CAP), -1, jnp.int32).at[block_ids, slot_index].set(pick_ids)
    slot_table = slot_table.reshape(block_count, EXPERTS, CAP)
    flat_gates = gate_weights.reshape(block_count, TOK_DEV * TOPK)

    def expert_step(accumulated, expert_index):
        sources = lax.dynamic_index_in_dim(slot_table, expert_index, 1, keepdims=False)
        safe_source = jnp.maximum(sources, 0)
        token_rows = (jnp.arange(block_count, dtype=jnp.int32)[:, None] * TOK_DEV + safe_source // TOPK).reshape(-1)
        live_rows = (sources >= 0).reshape(-1, 1)
        rows_in = jnp.where(live_rows, normed_two[token_rows], 0).astype(jnp.bfloat16)
        coords_in = jnp.where(live_rows, expert_coords[token_rows], 0).astype(jnp.bfloat16)
        gate_up = jnp.dot(rows_in, lax.dynamic_index_in_dim(expert_gate_up, expert_index, 0, keepdims=False), preferred_element_type=jnp.float32)
        adapter_bank = lax.dynamic_index_in_dim(adapter_expert_up, expert_index, 1, keepdims=False).reshape(ADAPTERS * RANK, FFE)
        up_part = gate_up[:, FFE:] + jnp.dot(coords_in, adapter_bank, preferred_element_type=jnp.float32)
        hidden = (jax.nn.relu(gate_up[:, :FFE]) * up_part).astype(jnp.bfloat16)
        outputs = jnp.dot(hidden, lax.dynamic_index_in_dim(expert_down, expert_index, 0, keepdims=False), preferred_element_type=jnp.float32).astype(jnp.bfloat16)
        outputs = lax.optimization_barrier(outputs).astype(jnp.float32)
        weight = jnp.take_along_axis(flat_gates, safe_source, axis=1).reshape(-1, 1)
        contribution = jnp.where(live_rows, weight * outputs, 0.0)
        return (accumulated.at[token_rows].add(contribution), None)
    combined = lax.scan(expert_step, jnp.zeros((TOKENS, D), jnp.float32), jnp.arange(EXPERTS, dtype=jnp.int32))[0]
    return (residual.astype(jnp.float32) + combined).astype(jnp.bfloat16)
```

```python
import jax
import jax.numpy as jnp
from jax import lax
from jax.sharding import PartitionSpec as P
from jax.experimental import pallas as pl
from jax.experimental.pallas import tpu as pltpu

HEADS = 12
KVH = 2
HD = 128
EXPERTS = 32
WINDOW = 4096
CAP = 64


EPSILON = 1e-06
NEGATIVE = -1e30


def scaled_norm(inputs, gain):
    floats = inputs.astype(jnp.float32)
    inverse = lax.rsqrt(jnp.mean(floats * floats, axis=-1, keepdims=True) + EPSILON)
    return (floats * inverse * gain).astype(jnp.bfloat16)


def segment_of(positions, lengths):
    seg_ends = jnp.cumsum(lengths)
    return jnp.sum((positions[:, None] >= seg_ends[None, :]).astype(jnp.int32), axis=1)


def adapter_select(token_adapter, adapter_count, rank_size):
    owners = jnp.repeat(jnp.arange(adapter_count, dtype=jnp.int32), rank_size)
    return token_adapter[:, None] == owners[None, :]


def low_coords(inputs, select, first_factor):
    adapter_count, inner_width, rank_size = first_factor.shape
    joined = jnp.transpose(first_factor, (1, 0, 2)).reshape(inner_width, adapter_count * rank_size)
    coords = jnp.dot(inputs, joined, preferred_element_type=jnp.float32)
    return jnp.where(select, coords, 0.0).astype(jnp.bfloat16)


def low_rank(inputs, select, first_factor, second_factor):
    coords = low_coords(inputs, select, first_factor)
    adapter_count, rank_size, outer_width = second_factor.shape
    return jnp.dot(
        coords,
        second_factor.reshape(adapter_count * rank_size, outer_width),
        preferred_element_type=jnp.float32,
    )


KEY_BLOCK = 512


def attention_kernel(first_ref, q_ref, k_ref, v_ref, qseg_ref, kseg_ref, init_ref, o_ref,
                     max_ref, sum_ref, acc_ref):
    j = pl.program_id(1)
    tok_rows = qseg_ref.shape[0]
    rows = q_ref.shape[1]
    group_size = rows // tok_rows
    first_pos = first_ref[0]
    low = jnp.maximum(first_pos - (WINDOW - 1), 0) // KEY_BLOCK
    high = (first_pos + tok_rows - 1) // KEY_BLOCK

    @pl.when(j == 0)
    def _():
        max_ref[...] = init_ref[0]
        sum_ref[...] = jnp.ones_like(sum_ref)
        acc_ref[...] = jnp.zeros_like(acc_ref)

    @pl.when(low + j <= high)
    def _():
        block = low + j
        scores = lax.dot_general(
            q_ref[0], k_ref[...], (((1,), (1,)), ((), ())),
            preferred_element_type=jnp.float32,
        ) * HD ** (-0.5)
        query_pos = first_pos + lax.broadcasted_iota(jnp.int32, (tok_rows, KEY_BLOCK), 0)
        key_pos = block * KEY_BLOCK + lax.broadcasted_iota(jnp.int32, (tok_rows, KEY_BLOCK), 1)
        key_seg = kseg_ref[...]
        allowed = (
            (key_pos <= query_pos)
            & (query_pos - key_pos < WINDOW)
            & ((key_seg == qseg_ref[...]) | (key_seg == 0))
        )
        scores = jnp.where(
            allowed[None], scores.reshape(group_size, tok_rows, KEY_BLOCK), NEGATIVE
        ).reshape(rows, KEY_BLOCK)
        prev_max = max_ref[...]
        new_max = jnp.maximum(prev_max, jnp.max(scores, axis=1, keepdims=True))
        factor = jnp.exp(prev_max - new_max)
        weights = jnp.exp(scores - new_max)
        sum_ref[...] = sum_ref[...] * factor + jnp.sum(weights, axis=1, keepdims=True)
        acc_ref[...] = acc_ref[...] * factor + jnp.dot(
            weights.astype(jnp.bfloat16), v_ref[...], preferred_element_type=jnp.float32
        )
        max_ref[...] = new_max

    @pl.when(j == pl.num_programs(1) - 1)
    def _():
        o_ref[0] = (acc_ref[...] / sum_ref[...]).astype(o_ref.dtype)


def window_attention(query_cols, key_piece, positions, segments, lengths, sink_logits):
    tok_rows = query_cols.shape[0]
    group_size = HEADS // KVH
    rows = group_size * tok_rows
    piece_rows = key_piece.shape[0]
    block_total = piece_rows // KEY_BLOCK
    steps = min(block_total, (WINDOW + tok_rows - 2) // KEY_BLOCK + 2)
    queries = jnp.transpose(
        query_cols.reshape(tok_rows, KVH, group_size, HD), (1, 2, 0, 3)
    ).reshape(KVH, rows, HD)
    key_seg = segment_of(jnp.arange(piece_rows, dtype=jnp.int32), lengths).reshape(1, piece_rows)
    query_seg = segments.reshape(tok_rows, 1)
    init = jnp.broadcast_to(
        sink_logits.reshape(KVH, group_size, 1, 1), (KVH, group_size, tok_rows, 1)
    ).reshape(KVH, rows, 1)
    first = positions[:1]

    def key_block(h, j, first_ref):
        f = first_ref[0]
        low = jnp.maximum(f - (WINDOW - 1), 0) // KEY_BLOCK
        high = (f + tok_rows - 1) // KEY_BLOCK
        return jnp.minimum(low + j, high)

    grid_spec = pltpu.PrefetchScalarGridSpec(
        num_scalar_prefetch=1,
        grid=(KVH, steps),
        in_specs=[
            pl.BlockSpec((1, rows, HD), lambda h, j, f: (h, 0, 0)),
            pl.BlockSpec((KEY_BLOCK, HD), lambda h, j, f: (key_block(h, j, f), h)),
            pl.BlockSpec((KEY_BLOCK, HD), lambda h, j, f: (key_block(h, j, f), KVH + h)),
            pl.BlockSpec((tok_rows, 1), lambda h, j, f: (0, 0)),
            pl.BlockSpec((1, KEY_BLOCK), lambda h, j, f: (0, key_block(h, j, f))),
            pl.BlockSpec((1, rows, 1), lambda h, j, f: (h, 0, 0)),
        ],
        out_specs=pl.BlockSpec((1, rows, HD), lambda h, j, f: (h, 0, 0)),
        scratch_shapes=[
            pltpu.VMEM((rows, 1), jnp.float32),
            pltpu.VMEM((rows, 1), jnp.float32),
            pltpu.VMEM((rows, HD), jnp.float32),
        ],
    )
    out = pl.pallas_call(
        attention_kernel,
        grid_spec=grid_spec,
        out_shape=jax.ShapeDtypeStruct((KVH, rows, HD), jnp.bfloat16),
        compiler_params=pltpu.CompilerParams(dimension_semantics=("arbitrary", "arbitrary")),
    )(first, queries, key_piece, key_piece, query_seg, key_seg, init)
    return jnp.transpose(
        out.reshape(KVH, group_size, tok_rows, HD), (2, 0, 1, 3)
    ).reshape(tok_rows, HEADS * HD)


def body(
    tokens,
    segment_lengths,
    segment_adapters,
    routes,
    gate_weights,
    attention_gain,
    attention_in,
    sink_logits,
    attention_out,
    expert_gain,
    expert_gate_up,
    expert_down,
    adapter_in_down,
    adapter_in_up,
    adapter_out_down,
    adapter_out_up,
    adapter_expert_down,
    adapter_expert_up,
):
    tok_rows = tokens.shape[0]
    lengths = segment_lengths[0]
    segment_total = lengths.shape[0]
    first_pos = lax.axis_index("exp") * tok_rows
    positions = first_pos + jnp.arange(tok_rows, dtype=jnp.int32)
    segments = segment_of(positions, lengths)
    matches = segments[:, None] == jnp.arange(segment_total, dtype=jnp.int32)[None, :]
    token_adapter = jnp.sum(jnp.where(matches, segment_adapters[0][None, :], 0), axis=1)
    held_factors = (
        lax.all_gather(adapter_in_down, "req", axis=0, tiled=True),
        lax.all_gather(adapter_in_up, "req", axis=0, tiled=True),
        lax.all_gather(adapter_out_down, "req", axis=0, tiled=True),
        lax.all_gather(adapter_out_up, "req", axis=0, tiled=True),
        lax.all_gather(adapter_expert_down, "req", axis=0, tiled=True),
        lax.all_gather(adapter_expert_up, "req", axis=0, tiled=True),
    )
    in_low, in_high, out_low, out_high, expert_low, expert_high = held_factors
    select = adapter_select(token_adapter, in_low.shape[0], in_low.shape[2])
    normed = scaled_norm(tokens, attention_gain)
    full_in, full_out = (
        lax.all_gather(attention_in, "req", axis=1, tiled=True),
        lax.all_gather(attention_out, "req", axis=1, tiled=True),
    )
    base_heads = jnp.dot(normed, full_in, preferred_element_type=jnp.float32)
    projected = (base_heads + low_rank(normed, select, in_low, in_high)).astype(jnp.bfloat16)
    group_size = HEADS // KVH
    key_value = projected[:, HEADS * HD :]
    key_piece = lax.all_gather(key_value, "exp", axis=0, tiled=True)
    attended = window_attention(
        projected[:, : HEADS * HD], key_piece, positions, segments, lengths, sink_logits
    )
    base_out = jnp.dot(attended, full_out, preferred_element_type=jnp.float32)
    residual = (
        tokens.astype(jnp.float32) + base_out + low_rank(attended, select, out_low, out_high)
    ).astype(jnp.bfloat16)
    normed_two = scaled_norm(residual, expert_gain)
    low_parts = low_coords(normed_two, select, expert_low)
    top_count = routes.shape[1]
    picked = routes.reshape(-1)
    expert_hot = (picked[:, None] == jnp.arange(EXPERTS, dtype=jnp.int32)[None, :]).astype(
        jnp.int32
    )
    arrival = jnp.sum((jnp.cumsum(expert_hot, axis=0) - 1) * expert_hot, axis=1)
    slot_index = picked * CAP + arrival
    pick_ids = jnp.arange(picked.shape[0], dtype=jnp.int32)
    sources = jnp.full((EXPERTS * CAP,), -1, jnp.int32).at[slot_index].set(pick_ids)
    filled = (sources >= 0)[:, None]
    token_rows = jnp.maximum(sources, 0) // top_count
    peer_count = lax.axis_size("exp")
    local_experts = EXPERTS // peer_count
    send_rows = jnp.where(filled, normed_two[token_rows], 0).reshape(
        peer_count, local_experts, CAP, -1
    )
    send_low = jnp.where(filled, low_parts[token_rows], 0).reshape(
        peer_count, local_experts, CAP, -1
    )
    adapter_bank = jnp.transpose(expert_high, (1, 0, 2, 3)).reshape(
        local_experts, -1, expert_high.shape[3]
    )
    arrived_rows = lax.all_to_all(send_rows, "exp", split_axis=0, concat_axis=0, tiled=True)
    arrived_low = lax.all_to_all(send_low, "exp", split_axis=0, concat_axis=0, tiled=True)
    hidden_width = expert_down.shape[1]
    gate_up = jnp.einsum(
        "necd,edf->necf", arrived_rows, expert_gate_up, preferred_element_type=jnp.float32
    )
    up_part = gate_up[..., hidden_width:] + jnp.einsum(
        "necr,erf->necf", arrived_low, adapter_bank, preferred_element_type=jnp.float32
    )
    hidden = (jax.nn.relu(gate_up[..., :hidden_width]) * up_part).astype(jnp.bfloat16)
    outputs = jnp.einsum(
        "necf,efd->necd", hidden, expert_down, preferred_element_type=jnp.float32
    ).astype(jnp.bfloat16)
    returned = lax.all_to_all(outputs, "exp", split_axis=0, concat_axis=0, tiled=True)
    flat_back = returned.reshape(EXPERTS * CAP, -1)
    per_pick = flat_back[slot_index].astype(jnp.float32).reshape(tok_rows, top_count, -1)
    combined = jnp.sum(gate_weights[:, :, None] * per_pick, axis=1)
    return (residual.astype(jnp.float32) + combined).astype(jnp.bfloat16)


def solution(mesh):
    return jax.shard_map(
        body,
        mesh=mesh,
        in_specs=(
            P(("req", "exp"), None),
            P("req", None),
            P("req", None),
            P(("req", "exp"), None),
            P(("req", "exp"), None),
            P(),
            P(None, "req"),
            P(),
            P(None, "req"),
            P(),
            P("exp", None, None),
            P("exp", None, None),
            P("req", None, None),
            P("req", None, None),
            P("req", None, None),
            P("req", None, None),
            P("req", None, None),
            P("req", "exp", None, None),
        ),
        out_specs=P(("req", "exp"), None),
        check_vma=False,
    )
```

```python
import jax
import jax.numpy as jnp
from jax import lax
from jax.sharding import PartitionSpec as P
from jax.experimental import pallas as pl
from jax.experimental.pallas import tpu as pltpu

HEADS = 12
KVH = 2
HD = 128
EXPERTS = 32
WINDOW = 4096
CAP = 64


EPSILON = 1e-06
NEGATIVE = -1e30


def scaled_norm(inputs, gain):
    floats = inputs.astype(jnp.float32)
    inverse = lax.rsqrt(jnp.mean(floats * floats, axis=-1, keepdims=True) + EPSILON)
    return (floats * inverse * gain).astype(jnp.bfloat16)


def segment_of(positions, lengths):
    seg_ends = jnp.cumsum(lengths)
    return jnp.sum((positions[:, None] >= seg_ends[None, :]).astype(jnp.int32), axis=1)


def adapter_select(token_adapter, adapter_count, rank_size):
    owners = jnp.repeat(jnp.arange(adapter_count, dtype=jnp.int32), rank_size)
    return token_adapter[:, None] == owners[None, :]


def low_coords(inputs, select, first_factor):
    adapter_count, inner_width, rank_size = first_factor.shape
    joined = jnp.transpose(first_factor, (1, 0, 2)).reshape(inner_width, adapter_count * rank_size)
    coords = jnp.dot(inputs, joined, preferred_element_type=jnp.float32)
    return jnp.where(select, coords, 0.0).astype(jnp.bfloat16)


def low_rank(inputs, select, first_factor, second_factor):
    coords = low_coords(inputs, select, first_factor)
    adapter_count, rank_size, outer_width = second_factor.shape
    return jnp.dot(
        coords,
        second_factor.reshape(adapter_count * rank_size, outer_width),
        preferred_element_type=jnp.float32,
    )


KEY_BLOCK = 512


def attention_kernel(first_ref, q_ref, k_ref, v_ref, qseg_ref, kseg_ref, init_ref, o_ref,
                     max_ref, sum_ref, acc_ref):
    j = pl.program_id(1)
    tok_rows = qseg_ref.shape[0]
    rows = q_ref.shape[1]
    group_size = rows // tok_rows
    first_pos = first_ref[0]
    low = jnp.maximum(first_pos - (WINDOW - 1), 0) // KEY_BLOCK
    high = (first_pos + tok_rows - 1) // KEY_BLOCK

    @pl.when(j == 0)
    def _():
        max_ref[...] = init_ref[0]
        sum_ref[...] = jnp.ones_like(sum_ref)
        acc_ref[...] = jnp.zeros_like(acc_ref)

    @pl.when(low + j <= high)
    def _():
        block = low + j
        scores = lax.dot_general(
            q_ref[0], k_ref[...], (((1,), (1,)), ((), ())),
            preferred_element_type=jnp.float32,
        ) * HD ** (-0.5)
        query_pos = first_pos + lax.broadcasted_iota(jnp.int32, (tok_rows, KEY_BLOCK), 0)
        key_pos = block * KEY_BLOCK + lax.broadcasted_iota(jnp.int32, (tok_rows, KEY_BLOCK), 1)
        key_seg = kseg_ref[...]
        allowed = (
            (key_pos <= query_pos)
            & (query_pos - key_pos < WINDOW)
            & ((key_seg == qseg_ref[...]) | (key_seg == 0))
        )
        scores = jnp.where(
            allowed[None], scores.reshape(group_size, tok_rows, KEY_BLOCK), NEGATIVE
        ).reshape(rows, KEY_BLOCK)
        prev_max = max_ref[...]
        new_max = jnp.maximum(prev_max, jnp.max(scores, axis=1, keepdims=True))
        factor = jnp.exp(prev_max - new_max)
        weights = jnp.exp(scores - new_max)
        sum_ref[...] = sum_ref[...] * factor + jnp.sum(weights, axis=1, keepdims=True)
        acc_ref[...] = acc_ref[...] * factor + jnp.dot(
            weights.astype(jnp.bfloat16), v_ref[...], preferred_element_type=jnp.float32
        )
        max_ref[...] = new_max

    @pl.when(j == pl.num_programs(1) - 1)
    def _():
        o_ref[0] = (acc_ref[...] / sum_ref[...]).astype(o_ref.dtype)


def window_attention(query_cols, key_piece, positions, segments, lengths, sink_logits):
    tok_rows = query_cols.shape[0]
    group_size = HEADS // KVH
    rows = group_size * tok_rows
    piece_rows = key_piece.shape[0]
    block_total = piece_rows // KEY_BLOCK
    steps = min(block_total, (WINDOW + tok_rows - 2) // KEY_BLOCK + 2)
    queries = jnp.transpose(
        query_cols.reshape(tok_rows, KVH, group_size, HD), (1, 2, 0, 3)
    ).reshape(KVH, rows, HD)
    key_seg = segment_of(jnp.arange(piece_rows, dtype=jnp.int32), lengths).reshape(1, piece_rows)
    query_seg = segments.reshape(tok_rows, 1)
    init = jnp.broadcast_to(
        sink_logits.reshape(KVH, group_size, 1, 1), (KVH, group_size, tok_rows, 1)
    ).reshape(KVH, rows, 1)
    first = positions[:1]

    def key_block(h, j, first_ref):
        f = first_ref[0]
        low = jnp.maximum(f - (WINDOW - 1), 0) // KEY_BLOCK
        high = (f + tok_rows - 1) // KEY_BLOCK
        return jnp.minimum(low + j, high)

    grid_spec = pltpu.PrefetchScalarGridSpec(
        num_scalar_prefetch=1,
        grid=(KVH, steps),
        in_specs=[
            pl.BlockSpec((1, rows, HD), lambda h, j, f: (h, 0, 0)),
            pl.BlockSpec((KEY_BLOCK, HD), lambda h, j, f: (key_block(h, j, f), h)),
            pl.BlockSpec((KEY_BLOCK, HD), lambda h, j, f: (key_block(h, j, f), KVH + h)),
            pl.BlockSpec((tok_rows, 1), lambda h, j, f: (0, 0)),
            pl.BlockSpec((1, KEY_BLOCK), lambda h, j, f: (0, key_block(h, j, f))),
            pl.BlockSpec((1, rows, 1), lambda h, j, f: (h, 0, 0)),
        ],
        out_specs=pl.BlockSpec((1, rows, HD), lambda h, j, f: (h, 0, 0)),
        scratch_shapes=[
            pltpu.VMEM((rows, 1), jnp.float32),
            pltpu.VMEM((rows, 1), jnp.float32),
            pltpu.VMEM((rows, HD), jnp.float32),
        ],
    )
    out = pl.pallas_call(
        attention_kernel,
        grid_spec=grid_spec,
        out_shape=jax.ShapeDtypeStruct((KVH, rows, HD), jnp.bfloat16),
        compiler_params=pltpu.CompilerParams(dimension_semantics=("arbitrary", "arbitrary")),
    )(first, queries, key_piece, key_piece, query_seg, key_seg, init)
    return jnp.transpose(
        out.reshape(KVH, group_size, tok_rows, HD), (2, 0, 1, 3)
    ).reshape(tok_rows, HEADS * HD)


def gather_factors(factors, axis_name):
    flat = jnp.concatenate([f.reshape(-1) for f in factors])
    gathered = lax.all_gather(flat, axis_name, axis=0, tiled=False)
    held = []
    offset = 0
    for f in factors:
        size = f.size
        piece = gathered[:, offset : offset + size].reshape((-1,) + f.shape[1:])
        held.append(piece)
        offset += size
    return tuple(held)


def body(
    tokens,
    segment_lengths,
    segment_adapters,
    routes,
    gate_weights,
    attention_gain,
    attention_in,
    sink_logits,
    attention_out,
    expert_gain,
    expert_gate_up,
    expert_down,
    adapter_in_down,
    adapter_in_up,
    adapter_out_down,
    adapter_out_up,
    adapter_expert_down,
    adapter_expert_up,
):
    tok_rows = tokens.shape[0]
    lengths = segment_lengths[0]
    segment_total = lengths.shape[0]
    first_pos = lax.axis_index("exp") * tok_rows
    positions = first_pos + jnp.arange(tok_rows, dtype=jnp.int32)
    segments = segment_of(positions, lengths)
    matches = segments[:, None] == jnp.arange(segment_total, dtype=jnp.int32)[None, :]
    token_adapter = jnp.sum(jnp.where(matches, segment_adapters[0][None, :], 0), axis=1)
    held_factors = gather_factors(
        (adapter_in_down, adapter_in_up, adapter_out_down, adapter_out_up,
         adapter_expert_down, adapter_expert_up),
        "req",
    )
    in_low, in_high, out_low, out_high, expert_low, expert_high = held_factors
    select = adapter_select(token_adapter, in_low.shape[0], in_low.shape[2])
    normed = scaled_norm(tokens, attention_gain)
    full_in, full_out = (
        lax.all_gather(attention_in, "req", axis=1, tiled=True),
        lax.all_gather(attention_out, "req", axis=1, tiled=True),
    )
    base_heads = jnp.dot(normed, full_in, preferred_element_type=jnp.float32)
    projected = (base_heads + low_rank(normed, select, in_low, in_high)).astype(jnp.bfloat16)
    group_size = HEADS // KVH
    key_value = projected[:, HEADS * HD :]
    key_piece = lax.all_gather(key_value, "exp", axis=0, tiled=True)
    attended = window_attention(
        projected[:, : HEADS * HD], key_piece, positions, segments, lengths, sink_logits
    )
    base_out = jnp.dot(attended, full_out, preferred_element_type=jnp.float32)
    residual = (
        tokens.astype(jnp.float32) + base_out + low_rank(attended, select, out_low, out_high)
    ).astype(jnp.bfloat16)
    normed_two = scaled_norm(residual, expert_gain)
    low_parts = low_coords(normed_two, select, expert_low)
    top_count = routes.shape[1]
    picked = routes.reshape(-1)
    expert_hot = (picked[:, None] == jnp.arange(EXPERTS, dtype=jnp.int32)[None, :]).astype(
        jnp.int32
    )
    arrival = jnp.sum((jnp.cumsum(expert_hot, axis=0) - 1) * expert_hot, axis=1)
    slot_index = picked * CAP + arrival
    slot_count = EXPERTS * CAP
    slot_ids = jnp.arange(slot_count, dtype=jnp.int32)
    token_slots = slot_index.reshape(tok_rows, top_count)
    dispatch = jnp.any(
        token_slots[None, :, :] == slot_ids[:, None, None], axis=2
    ).astype(jnp.bfloat16)
    peer_count = lax.axis_size("exp")
    local_experts = EXPERTS // peer_count
    row_width = normed_two.shape[1]
    send = jnp.dot(
        dispatch,
        jnp.concatenate([normed_two, low_parts], axis=1),
        preferred_element_type=jnp.float32,
    ).astype(jnp.bfloat16).reshape(peer_count, local_experts, CAP, -1)
    adapter_bank = jnp.transpose(expert_high, (1, 0, 2, 3)).reshape(
        local_experts, -1, expert_high.shape[3]
    )
    arrived = lax.all_to_all(send, "exp", split_axis=0, concat_axis=0, tiled=True)
    arrived_rows = arrived[..., :row_width]
    arrived_low = arrived[..., row_width:]
    hidden_width = expert_down.shape[1]
    gate_up = jnp.einsum(
        "necd,edf->necf", arrived_rows, expert_gate_up, preferred_element_type=jnp.float32
    )
    up_part = gate_up[..., hidden_width:] + jnp.einsum(
        "necr,erf->necf", arrived_low, adapter_bank, preferred_element_type=jnp.float32
    )
    hidden = (jax.nn.relu(gate_up[..., :hidden_width]) * up_part).astype(jnp.bfloat16)
    outputs = jnp.einsum(
        "necf,efd->necd", hidden, expert_down, preferred_element_type=jnp.float32
    ).astype(jnp.bfloat16)
    returned = lax.all_to_all(outputs, "exp", split_axis=0, concat_axis=0, tiled=True)
    flat_back = returned.reshape(EXPERTS * CAP, -1)
    gate_grid = jnp.sum(
        jnp.where(
            token_slots[:, :, None] == slot_ids[None, None, :], gate_weights[:, :, None], 0.0
        ),
        axis=1,
    )
    gate_high = gate_grid.astype(jnp.bfloat16)
    gate_low = (gate_grid - gate_high.astype(jnp.float32)).astype(jnp.bfloat16)
    combined = jnp.dot(gate_high, flat_back, preferred_element_type=jnp.float32) + jnp.dot(
        gate_low, flat_back, preferred_element_type=jnp.float32
    )
    return (residual.astype(jnp.float32) + combined).astype(jnp.bfloat16)


def solution(mesh):
    return jax.shard_map(
        body,
        mesh=mesh,
        in_specs=(
            P(("req", "exp"), None),
            P("req", None),
            P("req", None),
            P(("req", "exp"), None),
            P(("req", "exp"), None),
            P(),
            P(None, "req"),
            P(),
            P(None, "req"),
            P(),
            P("exp", None, None),
            P("exp", None, None),
            P("req", None, None),
            P("req", None, None),
            P("req", None, None),
            P("req", None, None),
            P("req", None, None),
            P("req", "exp", None, None),
        ),
        out_specs=P(("req", "exp"), None),
        check_vma=False,
    )
```

```python
import jax
import jax.numpy as jnp
from jax import lax
from jax.sharding import PartitionSpec as P
from jax.experimental import pallas as pl
from jax.experimental.pallas import tpu as pltpu

HEADS = 12
KVH = 2
HD = 128
EXPERTS = 32
WINDOW = 4096
CAP = 64


EPSILON = 1e-06
NEGATIVE = -1e30


def scaled_norm(inputs, gain):
    floats = inputs.astype(jnp.float32)
    inverse = lax.rsqrt(jnp.mean(floats * floats, axis=-1, keepdims=True) + EPSILON)
    return (floats * inverse * gain).astype(jnp.bfloat16)


def segment_of(positions, lengths):
    seg_ends = jnp.cumsum(lengths)
    return jnp.sum((positions[:, None] >= seg_ends[None, :]).astype(jnp.int32), axis=1)


def adapter_select(token_adapter, adapter_count, rank_size):
    owners = jnp.repeat(jnp.arange(adapter_count, dtype=jnp.int32), rank_size)
    return token_adapter[:, None] == owners[None, :]


def low_coords(inputs, select, joined):
    coords = jnp.dot(inputs, joined, preferred_element_type=jnp.float32)
    return jnp.where(select, coords, 0.0).astype(jnp.bfloat16)


def low_rank(inputs, select, joined, second):
    coords = low_coords(inputs, select, joined)
    return jnp.dot(coords, second, preferred_element_type=jnp.float32)


KEY_BLOCK = 512


def attention_kernel(first_ref, q_ref, k_ref, v_ref, qseg_ref, kseg_ref, init_ref, o_ref,
                     max_ref, sum_ref, acc_ref):
    j = pl.program_id(1)
    tok_rows = qseg_ref.shape[0]
    rows = q_ref.shape[1]
    group_size = rows // tok_rows
    first_pos = first_ref[0]
    low = jnp.maximum(first_pos - (WINDOW - 1), 0) // KEY_BLOCK
    high = (first_pos + tok_rows - 1) // KEY_BLOCK

    @pl.when(j == 0)
    def _():
        max_ref[...] = init_ref[0]
        sum_ref[...] = jnp.ones_like(sum_ref)
        acc_ref[...] = jnp.zeros_like(acc_ref)

    @pl.when(low + j <= high)
    def _():
        block = low + j
        scores = lax.dot_general(
            q_ref[0], k_ref[...], (((1,), (1,)), ((), ())),
            preferred_element_type=jnp.float32,
        ) * HD ** (-0.5)
        query_pos = first_pos + lax.broadcasted_iota(jnp.int32, (tok_rows, KEY_BLOCK), 0)
        key_pos = block * KEY_BLOCK + lax.broadcasted_iota(jnp.int32, (tok_rows, KEY_BLOCK), 1)
        key_seg = kseg_ref[...]
        allowed = (
            (key_pos <= query_pos)
            & (query_pos - key_pos < WINDOW)
            & ((key_seg == qseg_ref[...]) | (key_seg == 0))
        )
        scores = jnp.where(
            allowed[None], scores.reshape(group_size, tok_rows, KEY_BLOCK), NEGATIVE
        ).reshape(rows, KEY_BLOCK)
        prev_max = max_ref[...]
        new_max = jnp.maximum(prev_max, jnp.max(scores, axis=1, keepdims=True))
        factor = jnp.exp(prev_max - new_max)
        weights = jnp.exp(scores - new_max)
        sum_ref[...] = sum_ref[...] * factor + jnp.sum(weights, axis=1, keepdims=True)
        acc_ref[...] = acc_ref[...] * factor + jnp.dot(
            weights.astype(jnp.bfloat16), v_ref[...], preferred_element_type=jnp.float32
        )
        max_ref[...] = new_max

    @pl.when(j == pl.num_programs(1) - 1)
    def _():
        o_ref[0] = (acc_ref[...] / sum_ref[...]).astype(o_ref.dtype)


def window_attention(query_cols, key_piece, positions, segments, lengths, sink_logits):
    tok_rows = query_cols.shape[0]
    group_size = HEADS // KVH
    rows = group_size * tok_rows
    piece_rows = key_piece.shape[0]
    block_total = piece_rows // KEY_BLOCK
    steps = min(block_total, (WINDOW + tok_rows - 2) // KEY_BLOCK + 2)
    queries = jnp.transpose(
        query_cols.reshape(tok_rows, KVH, group_size, HD), (1, 2, 0, 3)
    ).reshape(KVH, rows, HD)
    key_seg = segment_of(jnp.arange(piece_rows, dtype=jnp.int32), lengths).reshape(1, piece_rows)
    query_seg = segments.reshape(tok_rows, 1)
    init = jnp.broadcast_to(
        sink_logits.reshape(KVH, group_size, 1, 1), (KVH, group_size, tok_rows, 1)
    ).reshape(KVH, rows, 1)
    first = positions[:1]

    def key_block(h, j, first_ref):
        f = first_ref[0]
        low = jnp.maximum(f - (WINDOW - 1), 0) // KEY_BLOCK
        high = (f + tok_rows - 1) // KEY_BLOCK
        return jnp.minimum(low + j, high)

    grid_spec = pltpu.PrefetchScalarGridSpec(
        num_scalar_prefetch=1,
        grid=(KVH, steps),
        in_specs=[
            pl.BlockSpec((1, rows, HD), lambda h, j, f: (h, 0, 0)),
            pl.BlockSpec((KEY_BLOCK, HD), lambda h, j, f: (key_block(h, j, f), h)),
            pl.BlockSpec((KEY_BLOCK, HD), lambda h, j, f: (key_block(h, j, f), KVH + h)),
            pl.BlockSpec((tok_rows, 1), lambda h, j, f: (0, 0)),
            pl.BlockSpec((1, KEY_BLOCK), lambda h, j, f: (0, key_block(h, j, f))),
            pl.BlockSpec((1, rows, 1), lambda h, j, f: (h, 0, 0)),
        ],
        out_specs=pl.BlockSpec((1, rows, HD), lambda h, j, f: (h, 0, 0)),
        scratch_shapes=[
            pltpu.VMEM((rows, 1), jnp.float32),
            pltpu.VMEM((rows, 1), jnp.float32),
            pltpu.VMEM((rows, HD), jnp.float32),
        ],
    )
    out = pl.pallas_call(
        attention_kernel,
        grid_spec=grid_spec,
        out_shape=jax.ShapeDtypeStruct((KVH, rows, HD), jnp.bfloat16),
        compiler_params=pltpu.CompilerParams(dimension_semantics=("arbitrary", "arbitrary")),
    )(first, queries, key_piece, key_piece, query_seg, key_seg, init)
    return jnp.transpose(
        out.reshape(KVH, group_size, tok_rows, HD), (2, 0, 1, 3)
    ).reshape(tok_rows, HEADS * HD)


def gather_weights(attention_in, downs, ups, expert_up, axis_name):
    inner_width = attention_in.shape[0]
    in_width = attention_in.shape[1]
    down_cols = [jnp.transpose(f, (1, 0, 2)).reshape(inner_width, -1) for f in downs]
    local_adapters, local_experts, rank_size, hidden_width = expert_up.shape
    up_rows = [f.reshape(-1, f.shape[2]) for f in ups] + [
        jnp.transpose(expert_up, (0, 2, 1, 3)).reshape(local_adapters * rank_size, -1)
    ]
    wide = lax.all_gather(
        jnp.concatenate([attention_in] + down_cols, axis=1), axis_name, axis=1, tiled=True
    )
    peers = wide.shape[1] // (in_width + sum(c.shape[1] for c in down_cols))
    wide = wide.reshape(inner_width, peers, -1)
    full_in = wide[:, :, :in_width].reshape(inner_width, -1)
    joined = []
    offset = in_width
    for c in down_cols:
        joined.append(wide[:, :, offset : offset + c.shape[1]].reshape(inner_width, -1))
        offset += c.shape[1]
    tall = lax.all_gather(jnp.concatenate(up_rows, axis=1), axis_name, axis=0, tiled=True)
    seconds = []
    offset = 0
    for r in up_rows:
        seconds.append(tall[:, offset : offset + r.shape[1]])
        offset += r.shape[1]
    bank = jnp.transpose(
        seconds[-1].reshape(tall.shape[0], local_experts, hidden_width), (1, 0, 2)
    )
    return full_in, joined, seconds[:-1], bank


def body(
    tokens,
    segment_lengths,
    segment_adapters,
    routes,
    gate_weights,
    attention_gain,
    attention_in,
    sink_logits,
    attention_out,
    expert_gain,
    expert_gate_up,
    expert_down,
    adapter_in_down,
    adapter_in_up,
    adapter_out_down,
    adapter_out_up,
    adapter_expert_down,
    adapter_expert_up,
):
    tok_rows = tokens.shape[0]
    lengths = segment_lengths[0]
    segment_total = lengths.shape[0]
    first_pos = lax.axis_index("exp") * tok_rows
    positions = first_pos + jnp.arange(tok_rows, dtype=jnp.int32)
    segments = segment_of(positions, lengths)
    matches = segments[:, None] == jnp.arange(segment_total, dtype=jnp.int32)[None, :]
    token_adapter = jnp.sum(jnp.where(matches, segment_adapters[0][None, :], 0), axis=1)
    adapter_count = adapter_in_down.shape[0] * lax.axis_size("req")
    rank_size = adapter_in_down.shape[2]
    select = adapter_select(token_adapter, adapter_count, rank_size)
    normed = scaled_norm(tokens, attention_gain)
    full_in, joined, seconds, adapter_bank = gather_weights(
        attention_in,
        (adapter_in_down, adapter_out_down, adapter_expert_down),
        (adapter_in_up, adapter_out_up),
        adapter_expert_up,
        "req",
    )
    in_low, out_low, expert_low = joined
    in_high, out_high = seconds
    full_out = lax.all_gather(attention_out, "req", axis=1, tiled=True)
    base_heads = jnp.dot(normed, full_in, preferred_element_type=jnp.float32)
    projected = (base_heads + low_rank(normed, select, in_low, in_high)).astype(jnp.bfloat16)
    group_size = HEADS // KVH
    key_value = projected[:, HEADS * HD :]
    key_piece = lax.all_gather(key_value, "exp", axis=0, tiled=True)
    attended = window_attention(
        projected[:, : HEADS * HD], key_piece, positions, segments, lengths, sink_logits
    )
    base_out = jnp.dot(attended, full_out, preferred_element_type=jnp.float32)
    residual = (
        tokens.astype(jnp.float32) + base_out + low_rank(attended, select, out_low, out_high)
    ).astype(jnp.bfloat16)
    normed_two = scaled_norm(residual, expert_gain)
    low_parts = low_coords(normed_two, select, expert_low)
    top_count = routes.shape[1]
    picked = routes.reshape(-1)
    expert_hot = (picked[:, None] == jnp.arange(EXPERTS, dtype=jnp.int32)[None, :]).astype(
        jnp.int32
    )
    arrival = jnp.sum((jnp.cumsum(expert_hot, axis=0) - 1) * expert_hot, axis=1)
    slot_index = picked * CAP + arrival
    slot_count = EXPERTS * CAP
    slot_ids = jnp.arange(slot_count, dtype=jnp.int32)
    token_slots = slot_index.reshape(tok_rows, top_count)
    dispatch = jnp.any(
        token_slots[None, :, :] == slot_ids[:, None, None], axis=2
    ).astype(jnp.bfloat16)
    peer_count = lax.axis_size("exp")
    local_experts = EXPERTS // peer_count
    row_width = normed_two.shape[1]
    send = jnp.dot(
        dispatch,
        jnp.concatenate([normed_two, low_parts], axis=1),
        preferred_element_type=jnp.float32,
    ).astype(jnp.bfloat16).reshape(peer_count, local_experts, CAP, -1)
    arrived = lax.all_to_all(send, "exp", split_axis=0, concat_axis=0, tiled=True)
    arrived_rows = arrived[..., :row_width]
    arrived_low = arrived[..., row_width:]
    hidden_width = expert_down.shape[1]
    gate_up = jnp.einsum(
        "necd,edf->necf", arrived_rows, expert_gate_up, preferred_element_type=jnp.float32
    )
    up_part = gate_up[..., hidden_width:] + jnp.einsum(
        "necr,erf->necf", arrived_low, adapter_bank, preferred_element_type=jnp.float32
    )
    hidden = (jax.nn.relu(gate_up[..., :hidden_width]) * up_part).astype(jnp.bfloat16)
    outputs = jnp.einsum(
        "necf,efd->necd", hidden, expert_down, preferred_element_type=jnp.float32
    ).astype(jnp.bfloat16)
    returned = lax.all_to_all(outputs, "exp", split_axis=0, concat_axis=0, tiled=True)
    flat_back = returned.reshape(EXPERTS * CAP, -1)
    gate_grid = jnp.sum(
        jnp.where(
            token_slots[:, :, None] == slot_ids[None, None, :], gate_weights[:, :, None], 0.0
        ),
        axis=1,
    )
    gate_high = gate_grid.astype(jnp.bfloat16)
    gate_low = (gate_grid - gate_high.astype(jnp.float32)).astype(jnp.bfloat16)
    combined = jnp.dot(gate_high, flat_back, preferred_element_type=jnp.float32) + jnp.dot(
        gate_low, flat_back, preferred_element_type=jnp.float32
    )
    return (residual.astype(jnp.float32) + combined).astype(jnp.bfloat16)


def solution(mesh):
    return jax.shard_map(
        body,
        mesh=mesh,
        in_specs=(
            P(("req", "exp"), None),
            P("req", None),
            P("req", None),
            P(("req", "exp"), None),
            P(("req", "exp"), None),
            P(),
            P(None, "req"),
            P(),
            P(None, "req"),
            P(),
            P("exp", None, None),
            P("exp", None, None),
            P("req", None, None),
            P("req", None, None),
            P("req", None, None),
            P("req", None, None),
            P("req", None, None),
            P("req", "exp", None, None),
        ),
        out_specs=P(("req", "exp"), None),
        check_vma=False,
    )
```

```python
import jax
import jax.numpy as jnp
from jax import lax
from jax.sharding import PartitionSpec as P
from jax.experimental import pallas as pl
from jax.experimental.pallas import tpu as pltpu

HEADS = 12
KVH = 2
HD = 128
EXPERTS = 32
WINDOW = 4096
CAP = 64


EPSILON = 1e-06
NEGATIVE = -1e30


def scaled_norm(inputs, gain):
    floats = inputs.astype(jnp.float32)
    inverse = lax.rsqrt(jnp.mean(floats * floats, axis=-1, keepdims=True) + EPSILON)
    return (floats * inverse * gain).astype(jnp.bfloat16)


def segment_of(positions, lengths):
    seg_ends = jnp.cumsum(lengths)
    return jnp.sum((positions[:, None] >= seg_ends[None, :]).astype(jnp.int32), axis=1)


def adapter_select(token_adapter, adapter_count, rank_size):
    owners = jnp.repeat(jnp.arange(adapter_count, dtype=jnp.int32), rank_size)
    return token_adapter[:, None] == owners[None, :]


def low_coords(inputs, select, joined):
    coords = jnp.dot(inputs, joined, preferred_element_type=jnp.float32)
    return jnp.where(select, coords, 0.0).astype(jnp.bfloat16)


def low_rank(inputs, select, joined, second):
    coords = low_coords(inputs, select, joined)
    return jnp.dot(coords, second, preferred_element_type=jnp.float32)


KEY_BLOCK = 512


def attention_kernel(first_ref, bmin_ref, bmax_ref, qrange_ref, q_ref, k_ref, v_ref, qseg_ref,
                     kseg_ref, init_ref, o_ref, max_ref, sum_ref, acc_ref):
    j = pl.program_id(1)
    tok_rows = qseg_ref.shape[0]
    rows = q_ref.shape[1]
    group_size = rows // tok_rows
    first_pos = first_ref[0]
    low = jnp.maximum(first_pos - (WINDOW - 1), 0) // KEY_BLOCK
    high = (first_pos + tok_rows - 1) // KEY_BLOCK

    @pl.when(j == 0)
    def _():
        max_ref[...] = init_ref[0]
        sum_ref[...] = jnp.ones_like(sum_ref)
        acc_ref[...] = jnp.zeros_like(acc_ref)

    block = jnp.minimum(low + j, high)
    seg_low = bmin_ref[block]
    seg_high = bmax_ref[block]
    shares_segment = (seg_low == 0) | (
        (seg_high >= qrange_ref[0]) & (seg_low <= qrange_ref[1])
    )

    @pl.when((low + j <= high) & shares_segment)
    def _():
        scores = lax.dot_general(
            q_ref[0], k_ref[...], (((1,), (1,)), ((), ())),
            preferred_element_type=jnp.float32,
        ) * HD ** (-0.5)
        query_pos = first_pos + lax.broadcasted_iota(jnp.int32, (tok_rows, KEY_BLOCK), 0)
        key_pos = block * KEY_BLOCK + lax.broadcasted_iota(jnp.int32, (tok_rows, KEY_BLOCK), 1)
        key_seg = kseg_ref[...]
        allowed = (
            (key_pos <= query_pos)
            & (query_pos - key_pos < WINDOW)
            & ((key_seg == qseg_ref[...]) | (key_seg == 0))
        )
        scores = jnp.where(
            allowed[None], scores.reshape(group_size, tok_rows, KEY_BLOCK), NEGATIVE
        ).reshape(rows, KEY_BLOCK)
        prev_max = max_ref[...]
        new_max = jnp.maximum(prev_max, jnp.max(scores, axis=1, keepdims=True))
        factor = jnp.exp(prev_max - new_max)
        weights = jnp.exp(scores - new_max)
        sum_ref[...] = sum_ref[...] * factor + jnp.sum(weights, axis=1, keepdims=True)
        acc_ref[...] = acc_ref[...] * factor + jnp.dot(
            weights.astype(jnp.bfloat16), v_ref[...], preferred_element_type=jnp.float32
        )
        max_ref[...] = new_max

    @pl.when(j == pl.num_programs(1) - 1)
    def _():
        o_ref[0] = (acc_ref[...] / sum_ref[...]).astype(o_ref.dtype)


def window_attention(query_cols, key_piece, positions, segments, lengths, sink_logits):
    tok_rows = query_cols.shape[0]
    group_size = HEADS // KVH
    rows = group_size * tok_rows
    piece_rows = key_piece.shape[0]
    block_total = piece_rows // KEY_BLOCK
    steps = min(block_total, (WINDOW + tok_rows - 2) // KEY_BLOCK + 2)
    queries = jnp.transpose(
        query_cols.reshape(tok_rows, KVH, group_size, HD), (1, 2, 0, 3)
    ).reshape(KVH, rows, HD)
    key_seg = segment_of(jnp.arange(piece_rows, dtype=jnp.int32), lengths).reshape(1, piece_rows)
    query_seg = segments.reshape(tok_rows, 1)
    init = jnp.broadcast_to(
        sink_logits.reshape(KVH, group_size, 1, 1), (KVH, group_size, tok_rows, 1)
    ).reshape(KVH, rows, 1)
    first = positions[:1]
    block_seg = key_seg.reshape(block_total, KEY_BLOCK)
    block_min = jnp.min(block_seg, axis=1)
    block_max = jnp.max(block_seg, axis=1)
    query_range = jnp.stack([segments[0], segments[-1]])

    def key_block(h, j, first_ref, *_):
        f = first_ref[0]
        low = jnp.maximum(f - (WINDOW - 1), 0) // KEY_BLOCK
        high = (f + tok_rows - 1) // KEY_BLOCK
        return jnp.minimum(low + j, high)

    grid_spec = pltpu.PrefetchScalarGridSpec(
        num_scalar_prefetch=4,
        grid=(KVH, steps),
        in_specs=[
            pl.BlockSpec((1, rows, HD), lambda h, j, f, *_: (h, 0, 0)),
            pl.BlockSpec((KEY_BLOCK, HD), lambda h, j, f, *_: (key_block(h, j, f), h)),
            pl.BlockSpec((KEY_BLOCK, HD), lambda h, j, f, *_: (key_block(h, j, f), KVH + h)),
            pl.BlockSpec((tok_rows, 1), lambda h, j, f, *_: (0, 0)),
            pl.BlockSpec((1, KEY_BLOCK), lambda h, j, f, *_: (0, key_block(h, j, f))),
            pl.BlockSpec((1, rows, 1), lambda h, j, f, *_: (h, 0, 0)),
        ],
        out_specs=pl.BlockSpec((1, rows, HD), lambda h, j, f, *_: (h, 0, 0)),
        scratch_shapes=[
            pltpu.VMEM((rows, 1), jnp.float32),
            pltpu.VMEM((rows, 1), jnp.float32),
            pltpu.VMEM((rows, HD), jnp.float32),
        ],
    )
    out = pl.pallas_call(
        attention_kernel,
        grid_spec=grid_spec,
        out_shape=jax.ShapeDtypeStruct((KVH, rows, HD), jnp.bfloat16),
        compiler_params=pltpu.CompilerParams(dimension_semantics=("arbitrary", "arbitrary")),
    )(first, block_min, block_max, query_range, queries, key_piece, key_piece, query_seg, key_seg, init)
    return jnp.transpose(
        out.reshape(KVH, group_size, tok_rows, HD), (2, 0, 1, 3)
    ).reshape(tok_rows, HEADS * HD)


def gather_weights(attention_in, downs, ups, expert_up, axis_name):
    inner_width = attention_in.shape[0]
    in_width = attention_in.shape[1]
    down_cols = [jnp.transpose(f, (1, 0, 2)).reshape(inner_width, -1) for f in downs]
    local_adapters, local_experts, rank_size, hidden_width = expert_up.shape
    up_rows = [f.reshape(-1, f.shape[2]) for f in ups] + [
        jnp.transpose(expert_up, (0, 2, 1, 3)).reshape(local_adapters * rank_size, -1)
    ]
    wide = lax.all_gather(
        jnp.concatenate([attention_in] + down_cols, axis=1), axis_name, axis=1, tiled=True
    )
    peers = wide.shape[1] // (in_width + sum(c.shape[1] for c in down_cols))
    wide = wide.reshape(inner_width, peers, -1)
    full_in = wide[:, :, :in_width].reshape(inner_width, -1)
    joined = []
    offset = in_width
    for c in down_cols:
        joined.append(wide[:, :, offset : offset + c.shape[1]].reshape(inner_width, -1))
        offset += c.shape[1]
    tall = lax.all_gather(jnp.concatenate(up_rows, axis=1), axis_name, axis=0, tiled=True)
    seconds = []
    offset = 0
    for r in up_rows:
        seconds.append(tall[:, offset : offset + r.shape[1]])
        offset += r.shape[1]
    bank = jnp.transpose(
        seconds[-1].reshape(tall.shape[0], local_experts, hidden_width), (1, 0, 2)
    )
    return full_in, joined, seconds[:-1], bank


def body(
    tokens,
    segment_lengths,
    segment_adapters,
    routes,
    gate_weights,
    attention_gain,
    attention_in,
    sink_logits,
    attention_out,
    expert_gain,
    expert_gate_up,
    expert_down,
    adapter_in_down,
    adapter_in_up,
    adapter_out_down,
    adapter_out_up,
    adapter_expert_down,
    adapter_expert_up,
):
    tok_rows = tokens.shape[0]
    lengths = segment_lengths[0]
    segment_total = lengths.shape[0]
    first_pos = lax.axis_index("exp") * tok_rows
    positions = first_pos + jnp.arange(tok_rows, dtype=jnp.int32)
    segments = segment_of(positions, lengths)
    matches = segments[:, None] == jnp.arange(segment_total, dtype=jnp.int32)[None, :]
    token_adapter = jnp.sum(jnp.where(matches, segment_adapters[0][None, :], 0), axis=1)
    adapter_count = adapter_in_down.shape[0] * lax.axis_size("req")
    rank_size = adapter_in_down.shape[2]
    select = adapter_select(token_adapter, adapter_count, rank_size)
    normed = scaled_norm(tokens, attention_gain)
    full_in, joined, seconds, adapter_bank = gather_weights(
        attention_in,
        (adapter_in_down, adapter_out_down, adapter_expert_down),
        (adapter_in_up, adapter_out_up),
        adapter_expert_up,
        "req",
    )
    in_low, out_low, expert_low = joined
    in_high, out_high = seconds
    full_out = lax.all_gather(attention_out, "req", axis=1, tiled=True)
    base_heads = jnp.dot(normed, full_in, preferred_element_type=jnp.float32)
    projected = (base_heads + low_rank(normed, select, in_low, in_high)).astype(jnp.bfloat16)
    group_size = HEADS // KVH
    key_value = projected[:, HEADS * HD :]
    key_piece = lax.all_gather(key_value, "exp", axis=0, tiled=True)
    attended = window_attention(
        projected[:, : HEADS * HD], key_piece, positions, segments, lengths, sink_logits
    )
    base_out = jnp.dot(attended, full_out, preferred_element_type=jnp.float32)
    residual = (
        tokens.astype(jnp.float32) + base_out + low_rank(attended, select, out_low, out_high)
    ).astype(jnp.bfloat16)
    normed_two = scaled_norm(residual, expert_gain)
    low_parts = low_coords(normed_two, select, expert_low)
    top_count = routes.shape[1]
    picked = routes.reshape(-1)
    expert_hot = (picked[:, None] == jnp.arange(EXPERTS, dtype=jnp.int32)[None, :]).astype(
        jnp.int32
    )
    arrival = jnp.sum((jnp.cumsum(expert_hot, axis=0) - 1) * expert_hot, axis=1)
    slot_index = picked * CAP + arrival
    slot_count = EXPERTS * CAP
    slot_ids = jnp.arange(slot_count, dtype=jnp.int32)
    token_slots = slot_index.reshape(tok_rows, top_count)
    dispatch = jnp.any(
        token_slots[None, :, :] == slot_ids[:, None, None], axis=2
    ).astype(jnp.bfloat16)
    peer_count = lax.axis_size("exp")
    local_experts = EXPERTS // peer_count
    row_width = normed_two.shape[1]
    send = jnp.dot(
        dispatch,
        jnp.concatenate([normed_two, low_parts], axis=1),
        preferred_element_type=jnp.float32,
    ).astype(jnp.bfloat16).reshape(peer_count, local_experts, CAP, -1)
    arrived = lax.all_to_all(send, "exp", split_axis=0, concat_axis=0, tiled=True)
    arrived_rows = arrived[..., :row_width]
    arrived_low = arrived[..., row_width:]
    hidden_width = expert_down.shape[1]
    gate_up = jnp.einsum(
        "necd,edf->necf", arrived_rows, expert_gate_up, preferred_element_type=jnp.float32
    )
    up_part = gate_up[..., hidden_width:] + jnp.einsum(
        "necr,erf->necf", arrived_low, adapter_bank, preferred_element_type=jnp.float32
    )
    hidden = (jax.nn.relu(gate_up[..., :hidden_width]) * up_part).astype(jnp.bfloat16)
    outputs = jnp.einsum(
        "necf,efd->necd", hidden, expert_down, preferred_element_type=jnp.float32
    ).astype(jnp.bfloat16)
    returned = lax.all_to_all(outputs, "exp", split_axis=0, concat_axis=0, tiled=True)
    flat_back = returned.reshape(EXPERTS * CAP, -1)
    gate_grid = jnp.sum(
        jnp.where(
            token_slots[:, :, None] == slot_ids[None, None, :], gate_weights[:, :, None], 0.0
        ),
        axis=1,
    )
    gate_high = gate_grid.astype(jnp.bfloat16)
    gate_low = (gate_grid - gate_high.astype(jnp.float32)).astype(jnp.bfloat16)
    combined = jnp.dot(gate_high, flat_back, preferred_element_type=jnp.float32) + jnp.dot(
        gate_low, flat_back, preferred_element_type=jnp.float32
    )
    return (residual.astype(jnp.float32) + combined).astype(jnp.bfloat16)


def solution(mesh):
    return jax.shard_map(
        body,
        mesh=mesh,
        in_specs=(
            P(("req", "exp"), None),
            P("req", None),
            P("req", None),
            P(("req", "exp"), None),
            P(("req", "exp"), None),
            P(),
            P(None, "req"),
            P(),
            P(None, "req"),
            P(),
            P("exp", None, None),
            P("exp", None, None),
            P("req", None, None),
            P("req", None, None),
            P("req", None, None),
            P("req", None, None),
            P("req", None, None),
            P("req", "exp", None, None),
        ),
        out_specs=P(("req", "exp"), None),
        check_vma=False,
    )
```

```python
import jax
import jax.numpy as jnp
from jax import lax
from jax.sharding import PartitionSpec as P
from jax.experimental import pallas as pl
from jax.experimental.pallas import tpu as pltpu

HEADS = 12
KVH = 2
HD = 128
EXPERTS = 32
WINDOW = 4096
CAP = 64


EPSILON = 1e-06
NEGATIVE = -1e30


def scaled_norm(inputs, gain):
    floats = inputs.astype(jnp.float32)
    inverse = lax.rsqrt(jnp.mean(floats * floats, axis=-1, keepdims=True) + EPSILON)
    return (floats * inverse * gain).astype(jnp.bfloat16)


def segment_of(positions, lengths):
    seg_ends = jnp.cumsum(lengths)
    return jnp.sum((positions[:, None] >= seg_ends[None, :]).astype(jnp.int32), axis=1)


def adapter_select(token_adapter, adapter_count, rank_size):
    owners = jnp.repeat(jnp.arange(adapter_count, dtype=jnp.int32), rank_size)
    return token_adapter[:, None] == owners[None, :]


def low_coords(inputs, select, joined):
    coords = jnp.dot(inputs, joined, preferred_element_type=jnp.float32)
    return jnp.where(select, coords, 0.0).astype(jnp.bfloat16)


def low_rank(inputs, select, joined, second):
    coords = low_coords(inputs, select, joined)
    return jnp.dot(coords, second, preferred_element_type=jnp.float32)


KEY_BLOCK = 512


def attention_kernel(first_ref, bmin_ref, bmax_ref, qrange_ref, q_ref, k_ref, v_ref, qseg_ref,
                     kseg_ref, init_ref, o_ref, max_ref, sum_ref, acc_ref):
    j = pl.program_id(1)
    tok_rows = qseg_ref.shape[0]
    rows = q_ref.shape[1]
    group_size = rows // tok_rows
    first_pos = first_ref[0]
    low = jnp.maximum(first_pos - (WINDOW - 1), 0) // KEY_BLOCK
    high = (first_pos + tok_rows - 1) // KEY_BLOCK

    @pl.when(j == 0)
    def _():
        max_ref[...] = init_ref[0]
        sum_ref[...] = jnp.ones_like(sum_ref)
        acc_ref[...] = jnp.zeros_like(acc_ref)

    block = jnp.minimum(low + j, high)
    seg_low = bmin_ref[block]
    seg_high = bmax_ref[block]
    shares_segment = (seg_low == 0) | (
        (seg_high >= qrange_ref[0]) & (seg_low <= qrange_ref[1])
    )

    @pl.when((low + j <= high) & shares_segment)
    def _():
        scores = lax.dot_general(
            q_ref[0], k_ref[...], (((1,), (1,)), ((), ())),
            preferred_element_type=jnp.float32,
        ) * HD ** (-0.5)
        query_pos = first_pos + lax.broadcasted_iota(jnp.int32, (tok_rows, KEY_BLOCK), 0)
        key_pos = block * KEY_BLOCK + lax.broadcasted_iota(jnp.int32, (tok_rows, KEY_BLOCK), 1)
        key_seg = kseg_ref[...]
        allowed = (
            (key_pos <= query_pos)
            & (query_pos - key_pos < WINDOW)
            & ((key_seg == qseg_ref[...]) | (key_seg == 0))
        )
        scores = jnp.where(
            allowed[None], scores.reshape(group_size, tok_rows, KEY_BLOCK), NEGATIVE
        ).reshape(rows, KEY_BLOCK)
        prev_max = max_ref[...]
        new_max = jnp.maximum(prev_max, jnp.max(scores, axis=1, keepdims=True))
        factor = jnp.exp(prev_max - new_max)
        weights = jnp.exp(scores - new_max)
        sum_ref[...] = sum_ref[...] * factor + jnp.sum(weights, axis=1, keepdims=True)
        acc_ref[...] = acc_ref[...] * factor + jnp.dot(
            weights.astype(jnp.bfloat16), v_ref[...], preferred_element_type=jnp.float32
        )
        max_ref[...] = new_max

    @pl.when(j == pl.num_programs(1) - 1)
    def _():
        o_ref[0] = (acc_ref[...] / sum_ref[...]).astype(o_ref.dtype)


def window_attention(query_cols, key_piece, positions, segments, lengths, sink_logits):
    tok_rows = query_cols.shape[0]
    group_size = HEADS // KVH
    rows = group_size * tok_rows
    piece_rows = key_piece.shape[0]
    block_total = piece_rows // KEY_BLOCK
    steps = min(block_total, (WINDOW + tok_rows - 2) // KEY_BLOCK + 2)
    queries = jnp.transpose(
        query_cols.reshape(tok_rows, KVH, group_size, HD), (1, 2, 0, 3)
    ).reshape(KVH, rows, HD)
    key_seg = segment_of(jnp.arange(piece_rows, dtype=jnp.int32), lengths).reshape(1, piece_rows)
    query_seg = segments.reshape(tok_rows, 1)
    init = jnp.broadcast_to(
        sink_logits.reshape(KVH, group_size, 1, 1), (KVH, group_size, tok_rows, 1)
    ).reshape(KVH, rows, 1)
    first = positions[:1]
    block_seg = key_seg.reshape(block_total, KEY_BLOCK)
    block_min = jnp.min(block_seg, axis=1)
    block_max = jnp.max(block_seg, axis=1)
    query_range = jnp.stack([segments[0], segments[-1]])

    def key_block(h, j, first_ref, *_):
        f = first_ref[0]
        low = jnp.maximum(f - (WINDOW - 1), 0) // KEY_BLOCK
        high = (f + tok_rows - 1) // KEY_BLOCK
        return jnp.minimum(low + j, high)

    grid_spec = pltpu.PrefetchScalarGridSpec(
        num_scalar_prefetch=4,
        grid=(KVH, steps),
        in_specs=[
            pl.BlockSpec((1, rows, HD), lambda h, j, f, *_: (h, 0, 0)),
            pl.BlockSpec((KEY_BLOCK, HD), lambda h, j, f, *_: (key_block(h, j, f), h)),
            pl.BlockSpec((KEY_BLOCK, HD), lambda h, j, f, *_: (key_block(h, j, f), KVH + h)),
            pl.BlockSpec((tok_rows, 1), lambda h, j, f, *_: (0, 0)),
            pl.BlockSpec((1, KEY_BLOCK), lambda h, j, f, *_: (0, key_block(h, j, f))),
            pl.BlockSpec((1, rows, 1), lambda h, j, f, *_: (h, 0, 0)),
        ],
        out_specs=pl.BlockSpec((1, rows, HD), lambda h, j, f, *_: (h, 0, 0)),
        scratch_shapes=[
            pltpu.VMEM((rows, 1), jnp.float32),
            pltpu.VMEM((rows, 1), jnp.float32),
            pltpu.VMEM((rows, HD), jnp.float32),
        ],
    )
    out = pl.pallas_call(
        attention_kernel,
        grid_spec=grid_spec,
        out_shape=jax.ShapeDtypeStruct((KVH, rows, HD), jnp.bfloat16),
        compiler_params=pltpu.CompilerParams(dimension_semantics=("arbitrary", "arbitrary")),
    )(first, block_min, block_max, query_range, queries, key_piece, key_piece, query_seg, key_seg, init)
    return jnp.transpose(
        out.reshape(KVH, group_size, tok_rows, HD), (2, 0, 1, 3)
    ).reshape(tok_rows, HEADS * HD)


def gather_columns(first, downs, axis_name):
    inner_width = first.shape[0]
    first_width = first.shape[1]
    down_cols = [jnp.transpose(f, (1, 0, 2)).reshape(inner_width, -1) for f in downs]
    wide = lax.all_gather(
        jnp.concatenate([first] + down_cols, axis=1), axis_name, axis=1, tiled=True
    )
    peers = wide.shape[1] // (first_width + sum(c.shape[1] for c in down_cols))
    wide = wide.reshape(inner_width, peers, -1)
    held = [wide[:, :, :first_width].reshape(inner_width, -1)]
    offset = first_width
    for c in down_cols:
        held.append(wide[:, :, offset : offset + c.shape[1]].reshape(inner_width, -1))
        offset += c.shape[1]
    return held


def gather_rows(rows, axis_name):
    tall = lax.all_gather(jnp.concatenate(rows, axis=1), axis_name, axis=0, tiled=True)
    held = []
    offset = 0
    for r in rows:
        held.append(tall[:, offset : offset + r.shape[1]])
        offset += r.shape[1]
    return held


def body(
    tokens,
    segment_lengths,
    segment_adapters,
    routes,
    gate_weights,
    attention_gain,
    attention_in,
    sink_logits,
    attention_out,
    expert_gain,
    expert_gate_up,
    expert_down,
    adapter_in_down,
    adapter_in_up,
    adapter_out_down,
    adapter_out_up,
    adapter_expert_down,
    adapter_expert_up,
):
    tok_rows = tokens.shape[0]
    lengths = segment_lengths[0]
    segment_total = lengths.shape[0]
    first_pos = lax.axis_index("exp") * tok_rows
    positions = first_pos + jnp.arange(tok_rows, dtype=jnp.int32)
    segments = segment_of(positions, lengths)
    matches = segments[:, None] == jnp.arange(segment_total, dtype=jnp.int32)[None, :]
    token_adapter = jnp.sum(jnp.where(matches, segment_adapters[0][None, :], 0), axis=1)
    adapter_count = adapter_in_down.shape[0] * lax.axis_size("req")
    rank_size = adapter_in_down.shape[2]
    select = adapter_select(token_adapter, adapter_count, rank_size)
    normed = scaled_norm(tokens, attention_gain)
    full_in, in_low = gather_columns(attention_in, (adapter_in_down,), "req")
    (in_high,) = gather_rows((adapter_in_up.reshape(-1, adapter_in_up.shape[2]),), "req")
    base_heads = jnp.dot(normed, full_in, preferred_element_type=jnp.float32)
    projected = (base_heads + low_rank(normed, select, in_low, in_high)).astype(jnp.bfloat16)
    group_size = HEADS // KVH
    key_value = projected[:, HEADS * HD :]
    key_piece = lax.all_gather(key_value, "exp", axis=0, tiled=True)
    late_factors = (
        attention_out, adapter_out_down, adapter_expert_down, adapter_out_up, adapter_expert_up
    )
    late_factors, key_piece = lax.optimization_barrier((late_factors, key_piece))
    attention_out, adapter_out_down, adapter_expert_down, adapter_out_up, adapter_expert_up = (
        late_factors
    )
    full_out, out_low, expert_low = gather_columns(
        attention_out, (adapter_out_down, adapter_expert_down), "req"
    )
    local_adapters, local_experts, _, hidden_width = adapter_expert_up.shape
    out_high, bank_rows = gather_rows(
        (
            adapter_out_up.reshape(-1, adapter_out_up.shape[2]),
            jnp.transpose(adapter_expert_up, (0, 2, 1, 3)).reshape(local_adapters * rank_size, -1),
        ),
        "req",
    )
    adapter_bank = jnp.transpose(
        bank_rows.reshape(bank_rows.shape[0], local_experts, hidden_width), (1, 0, 2)
    )
    attended = window_attention(
        projected[:, : HEADS * HD], key_piece, positions, segments, lengths, sink_logits
    )
    base_out = jnp.dot(attended, full_out, preferred_element_type=jnp.float32)
    residual = (
        tokens.astype(jnp.float32) + base_out + low_rank(attended, select, out_low, out_high)
    ).astype(jnp.bfloat16)
    normed_two = scaled_norm(residual, expert_gain)
    low_parts = low_coords(normed_two, select, expert_low)
    top_count = routes.shape[1]
    picked = routes.reshape(-1)
    expert_hot = (picked[:, None] == jnp.arange(EXPERTS, dtype=jnp.int32)[None, :]).astype(
        jnp.int32
    )
    arrival = jnp.sum((jnp.cumsum(expert_hot, axis=0) - 1) * expert_hot, axis=1)
    slot_index = picked * CAP + arrival
    slot_count = EXPERTS * CAP
    slot_ids = jnp.arange(slot_count, dtype=jnp.int32)
    token_slots = slot_index.reshape(tok_rows, top_count)
    dispatch = jnp.any(
        token_slots[None, :, :] == slot_ids[:, None, None], axis=2
    ).astype(jnp.bfloat16)
    peer_count = lax.axis_size("exp")
    local_experts = EXPERTS // peer_count
    row_width = normed_two.shape[1]
    send = jnp.dot(
        dispatch,
        jnp.concatenate([normed_two, low_parts], axis=1),
        preferred_element_type=jnp.float32,
    ).astype(jnp.bfloat16).reshape(peer_count, local_experts, CAP, -1)
    arrived = lax.all_to_all(send, "exp", split_axis=0, concat_axis=0, tiled=True)
    arrived_rows = arrived[..., :row_width]
    arrived_low = arrived[..., row_width:]
    hidden_width = expert_down.shape[1]
    gate_up = jnp.einsum(
        "necd,edf->necf", arrived_rows, expert_gate_up, preferred_element_type=jnp.float32
    )
    up_part = gate_up[..., hidden_width:] + jnp.einsum(
        "necr,erf->necf", arrived_low, adapter_bank, preferred_element_type=jnp.float32
    )
    hidden = (jax.nn.relu(gate_up[..., :hidden_width]) * up_part).astype(jnp.bfloat16)
    outputs = jnp.einsum(
        "necf,efd->necd", hidden, expert_down, preferred_element_type=jnp.float32
    ).astype(jnp.bfloat16)
    returned = lax.all_to_all(outputs, "exp", split_axis=0, concat_axis=0, tiled=True)
    flat_back = returned.reshape(EXPERTS * CAP, -1)
    gate_grid = jnp.sum(
        jnp.where(
            token_slots[:, :, None] == slot_ids[None, None, :], gate_weights[:, :, None], 0.0
        ),
        axis=1,
    )
    gate_high = gate_grid.astype(jnp.bfloat16)
    gate_low = (gate_grid - gate_high.astype(jnp.float32)).astype(jnp.bfloat16)
    combined = jnp.dot(gate_high, flat_back, preferred_element_type=jnp.float32) + jnp.dot(
        gate_low, flat_back, preferred_element_type=jnp.float32
    )
    return (residual.astype(jnp.float32) + combined).astype(jnp.bfloat16)


def solution(mesh):
    return jax.shard_map(
        body,
        mesh=mesh,
        in_specs=(
            P(("req", "exp"), None),
            P("req", None),
            P("req", None),
            P(("req", "exp"), None),
            P(("req", "exp"), None),
            P(),
            P(None, "req"),
            P(),
            P(None, "req"),
            P(),
            P("exp", None, None),
            P("exp", None, None),
            P("req", None, None),
            P("req", None, None),
            P("req", None, None),
            P("req", None, None),
            P("req", None, None),
            P("req", "exp", None, None),
        ),
        out_specs=P(("req", "exp"), None),
        check_vma=False,
    )
```

```python
import jax
import jax.numpy as jnp
from jax import lax
from jax.sharding import PartitionSpec as P
from jax.experimental import pallas as pl
from jax.experimental.pallas import tpu as pltpu

HEADS = 12
KVH = 2
HD = 128
EXPERTS = 32
WINDOW = 4096
CAP = 64


EPSILON = 1e-06
NEGATIVE = -1e30


def scaled_norm(inputs, gain):
    floats = inputs.astype(jnp.float32)
    inverse = lax.rsqrt(jnp.mean(floats * floats, axis=-1, keepdims=True) + EPSILON)
    return (floats * inverse * gain).astype(jnp.bfloat16)


def segment_of(positions, lengths):
    seg_ends = jnp.cumsum(lengths)
    return jnp.sum((positions[:, None] >= seg_ends[None, :]).astype(jnp.int32), axis=1)


def adapter_select(token_adapter, adapter_count, rank_size):
    owners = jnp.repeat(jnp.arange(adapter_count, dtype=jnp.int32), rank_size)
    return token_adapter[:, None] == owners[None, :]


def low_coords(inputs, select, joined):
    coords = jnp.dot(inputs, joined, preferred_element_type=jnp.float32)
    return jnp.where(select, coords, 0.0).astype(jnp.bfloat16)


def low_rank(inputs, select, joined, second):
    coords = low_coords(inputs, select, joined)
    return jnp.dot(coords, second, preferred_element_type=jnp.float32)


KEY_BLOCK = 512


def attention_kernel(first_ref, bmin_ref, bmax_ref, qrange_ref, q_ref, k_ref, v_ref, qseg_ref,
                     kseg_ref, init_ref, o_ref, max_ref, sum_ref, acc_ref):
    j = pl.program_id(1)
    tok_rows = qseg_ref.shape[0]
    rows = q_ref.shape[1]
    group_size = rows // tok_rows
    first_pos = first_ref[0]
    low = jnp.maximum(first_pos - (WINDOW - 1), 0) // KEY_BLOCK
    high = (first_pos + tok_rows - 1) // KEY_BLOCK

    @pl.when(j == 0)
    def _():
        max_ref[...] = init_ref[0]
        sum_ref[...] = jnp.ones_like(sum_ref)
        acc_ref[...] = jnp.zeros_like(acc_ref)

    block = jnp.minimum(low + j, high)
    seg_low = bmin_ref[block]
    seg_high = bmax_ref[block]
    shares_segment = (seg_low == 0) | (
        (seg_high >= qrange_ref[0]) & (seg_low <= qrange_ref[1])
    )

    @pl.when((low + j <= high) & shares_segment)
    def _():
        scores = lax.dot_general(
            q_ref[0], k_ref[...], (((1,), (1,)), ((), ())),
            preferred_element_type=jnp.float32,
        ) * HD ** (-0.5)
        query_pos = first_pos + lax.broadcasted_iota(jnp.int32, (tok_rows, KEY_BLOCK), 0)
        key_pos = block * KEY_BLOCK + lax.broadcasted_iota(jnp.int32, (tok_rows, KEY_BLOCK), 1)
        key_seg = kseg_ref[...]
        allowed = (
            (key_pos <= query_pos)
            & (query_pos - key_pos < WINDOW)
            & ((key_seg == qseg_ref[...]) | (key_seg == 0))
        )
        scores = jnp.where(
            allowed[None], scores.reshape(group_size, tok_rows, KEY_BLOCK), NEGATIVE
        ).reshape(rows, KEY_BLOCK)
        prev_max = max_ref[...]
        new_max = jnp.maximum(prev_max, jnp.max(scores, axis=1, keepdims=True))
        factor = jnp.exp(prev_max - new_max)
        weights = jnp.exp(scores - new_max)
        sum_ref[...] = sum_ref[...] * factor + jnp.sum(weights, axis=1, keepdims=True)
        acc_ref[...] = acc_ref[...] * factor + jnp.dot(
            weights.astype(jnp.bfloat16), v_ref[...], preferred_element_type=jnp.float32
        )
        max_ref[...] = new_max

    @pl.when(j == pl.num_programs(1) - 1)
    def _():
        o_ref[0] = (acc_ref[...] / sum_ref[...]).astype(o_ref.dtype)


def window_attention(query_cols, key_piece, positions, segments, lengths, sink_logits):
    tok_rows = query_cols.shape[0]
    group_size = HEADS // KVH
    rows = group_size * tok_rows
    piece_rows = key_piece.shape[0]
    block_total = piece_rows // KEY_BLOCK
    steps = min(block_total, (WINDOW + tok_rows - 2) // KEY_BLOCK + 2)
    queries = jnp.transpose(
        query_cols.reshape(tok_rows, KVH, group_size, HD), (1, 2, 0, 3)
    ).reshape(KVH, rows, HD)
    key_seg = segment_of(jnp.arange(piece_rows, dtype=jnp.int32), lengths).reshape(1, piece_rows)
    query_seg = segments.reshape(tok_rows, 1)
    init = jnp.broadcast_to(
        sink_logits.reshape(KVH, group_size, 1, 1), (KVH, group_size, tok_rows, 1)
    ).reshape(KVH, rows, 1)
    first = positions[:1]
    block_seg = key_seg.reshape(block_total, KEY_BLOCK)
    block_min = jnp.min(block_seg, axis=1)
    block_max = jnp.max(block_seg, axis=1)
    query_range = jnp.stack([segments[0], segments[-1]])

    def key_block(h, j, first_ref, *_):
        f = first_ref[0]
        low = jnp.maximum(f - (WINDOW - 1), 0) // KEY_BLOCK
        high = (f + tok_rows - 1) // KEY_BLOCK
        return jnp.minimum(low + j, high)

    grid_spec = pltpu.PrefetchScalarGridSpec(
        num_scalar_prefetch=4,
        grid=(KVH, steps),
        in_specs=[
            pl.BlockSpec((1, rows, HD), lambda h, j, f, *_: (h, 0, 0)),
            pl.BlockSpec((KEY_BLOCK, HD), lambda h, j, f, *_: (key_block(h, j, f), h)),
            pl.BlockSpec((KEY_BLOCK, HD), lambda h, j, f, *_: (key_block(h, j, f), KVH + h)),
            pl.BlockSpec((tok_rows, 1), lambda h, j, f, *_: (0, 0)),
            pl.BlockSpec((1, KEY_BLOCK), lambda h, j, f, *_: (0, key_block(h, j, f))),
            pl.BlockSpec((1, rows, 1), lambda h, j, f, *_: (h, 0, 0)),
        ],
        out_specs=pl.BlockSpec((1, rows, HD), lambda h, j, f, *_: (h, 0, 0)),
        scratch_shapes=[
            pltpu.VMEM((rows, 1), jnp.float32),
            pltpu.VMEM((rows, 1), jnp.float32),
            pltpu.VMEM((rows, HD), jnp.float32),
        ],
    )
    out = pl.pallas_call(
        attention_kernel,
        grid_spec=grid_spec,
        out_shape=jax.ShapeDtypeStruct((KVH, rows, HD), jnp.bfloat16),
        compiler_params=pltpu.CompilerParams(dimension_semantics=("arbitrary", "arbitrary")),
    )(first, block_min, block_max, query_range, queries, key_piece, key_piece, query_seg, key_seg, init)
    return jnp.transpose(
        out.reshape(KVH, group_size, tok_rows, HD), (2, 0, 1, 3)
    ).reshape(tok_rows, HEADS * HD)


def gather_weights(attention_in, downs, ups, expert_up, axis_name):
    inner_width = attention_in.shape[0]
    in_width = attention_in.shape[1]
    down_cols = [jnp.transpose(f, (1, 0, 2)).reshape(inner_width, -1) for f in downs]
    local_adapters, local_experts, rank_size, hidden_width = expert_up.shape
    up_rows = [f.reshape(-1, f.shape[2]) for f in ups] + [
        jnp.transpose(expert_up, (0, 2, 1, 3)).reshape(local_adapters * rank_size, -1)
    ]
    wide = lax.all_gather(
        jnp.concatenate([attention_in] + down_cols, axis=1), axis_name, axis=1, tiled=True
    )
    peers = wide.shape[1] // (in_width + sum(c.shape[1] for c in down_cols))
    wide = wide.reshape(inner_width, peers, -1)
    full_in = wide[:, :, :in_width].reshape(inner_width, -1)
    joined = []
    offset = in_width
    for c in down_cols:
        joined.append(wide[:, :, offset : offset + c.shape[1]].reshape(inner_width, -1))
        offset += c.shape[1]
    tall = lax.all_gather(jnp.concatenate(up_rows, axis=1), axis_name, axis=0, tiled=True)
    seconds = []
    offset = 0
    for r in up_rows:
        seconds.append(tall[:, offset : offset + r.shape[1]])
        offset += r.shape[1]
    bank = jnp.transpose(
        seconds[-1].reshape(tall.shape[0], local_experts, hidden_width), (1, 0, 2)
    )
    return full_in, joined, seconds[:-1], bank


def body(
    tokens,
    segment_lengths,
    segment_adapters,
    routes,
    gate_weights,
    attention_gain,
    attention_in,
    sink_logits,
    attention_out,
    expert_gain,
    expert_gate_up,
    expert_down,
    adapter_in_down,
    adapter_in_up,
    adapter_out_down,
    adapter_out_up,
    adapter_expert_down,
    adapter_expert_up,
):
    tok_rows = tokens.shape[0]
    lengths = segment_lengths[0]
    segment_total = lengths.shape[0]
    first_pos = lax.axis_index("exp") * tok_rows
    positions = first_pos + jnp.arange(tok_rows, dtype=jnp.int32)
    segments = segment_of(positions, lengths)
    matches = segments[:, None] == jnp.arange(segment_total, dtype=jnp.int32)[None, :]
    token_adapter = jnp.sum(jnp.where(matches, segment_adapters[0][None, :], 0), axis=1)
    adapter_count = adapter_in_down.shape[0] * lax.axis_size("req")
    rank_size = adapter_in_down.shape[2]
    select = adapter_select(token_adapter, adapter_count, rank_size)
    normed = scaled_norm(tokens, attention_gain)
    full_in, joined, seconds, adapter_bank = gather_weights(
        attention_in,
        (adapter_in_down, adapter_out_down, adapter_expert_down),
        (adapter_in_up, adapter_out_up),
        adapter_expert_up,
        "req",
    )
    in_low, out_low, expert_low = joined
    in_high, out_high = seconds
    full_out = lax.all_gather(attention_out, "req", axis=1, tiled=True)
    base_heads = jnp.dot(normed, full_in, preferred_element_type=jnp.float32)
    projected = (base_heads + low_rank(normed, select, in_low, in_high)).astype(jnp.bfloat16)
    group_size = HEADS // KVH
    key_value = projected[:, HEADS * HD :]
    key_piece = lax.all_gather(key_value, "exp", axis=0, tiled=True)
    attended = window_attention(
        projected[:, : HEADS * HD], key_piece, positions, segments, lengths, sink_logits
    )
    base_out = jnp.dot(attended, full_out, preferred_element_type=jnp.float32)
    residual = (
        tokens.astype(jnp.float32) + base_out + low_rank(attended, select, out_low, out_high)
    ).astype(jnp.bfloat16)
    normed_two = scaled_norm(residual, expert_gain)
    low_parts = low_coords(normed_two, select, expert_low)
    top_count = routes.shape[1]
    picked = routes.reshape(-1)
    expert_hot = (picked[:, None] == jnp.arange(EXPERTS, dtype=jnp.int32)[None, :]).astype(
        jnp.int32
    )
    arrival = jnp.sum((jnp.cumsum(expert_hot, axis=0) - 1) * expert_hot, axis=1)
    slot_index = picked * CAP + arrival
    slot_count = EXPERTS * CAP
    slot_ids = jnp.arange(slot_count, dtype=jnp.int32)
    token_slots = slot_index.reshape(tok_rows, top_count)
    dispatch = jnp.any(
        token_slots[None, :, :] == slot_ids[:, None, None], axis=2
    ).astype(jnp.bfloat16)
    peer_count = lax.axis_size("exp")
    local_experts = EXPERTS // peer_count
    row_width = normed_two.shape[1]
    send = jnp.dot(
        dispatch,
        jnp.concatenate([normed_two, low_parts], axis=1),
        preferred_element_type=jnp.float32,
    ).astype(jnp.bfloat16).reshape(peer_count, local_experts, CAP, -1)
    hidden_width = expert_down.shape[1]

    def expert_chunk(chunk):
        arrived = lax.all_to_all(chunk, "exp", split_axis=0, concat_axis=0, tiled=True)
        arrived_rows = arrived[..., :row_width]
        arrived_low = arrived[..., row_width:]
        gate_up = jnp.einsum(
            "necd,edf->necf", arrived_rows, expert_gate_up, preferred_element_type=jnp.float32
        )
        up_part = gate_up[..., hidden_width:] + jnp.einsum(
            "necr,erf->necf", arrived_low, adapter_bank, preferred_element_type=jnp.float32
        )
        hidden = (jax.nn.relu(gate_up[..., :hidden_width]) * up_part).astype(jnp.bfloat16)
        outputs = jnp.einsum(
            "necf,efd->necd", hidden, expert_down, preferred_element_type=jnp.float32
        ).astype(jnp.bfloat16)
        return lax.all_to_all(outputs, "exp", split_axis=0, concat_axis=0, tiled=True)

    half = CAP // 2
    returned = jnp.concatenate(
        [expert_chunk(send[:, :, :half]), expert_chunk(send[:, :, half:])], axis=2
    )
    flat_back = returned.reshape(EXPERTS * CAP, -1)
    gate_grid = jnp.sum(
        jnp.where(
            token_slots[:, :, None] == slot_ids[None, None, :], gate_weights[:, :, None], 0.0
        ),
        axis=1,
    )
    gate_high = gate_grid.astype(jnp.bfloat16)
    gate_low = (gate_grid - gate_high.astype(jnp.float32)).astype(jnp.bfloat16)
    combined = jnp.dot(gate_high, flat_back, preferred_element_type=jnp.float32) + jnp.dot(
        gate_low, flat_back, preferred_element_type=jnp.float32
    )
    return (residual.astype(jnp.float32) + combined).astype(jnp.bfloat16)


def solution(mesh):
    return jax.shard_map(
        body,
        mesh=mesh,
        in_specs=(
            P(("req", "exp"), None),
            P("req", None),
            P("req", None),
            P(("req", "exp"), None),
            P(("req", "exp"), None),
            P(),
            P(None, "req"),
            P(),
            P(None, "req"),
            P(),
            P("exp", None, None),
            P("exp", None, None),
            P("req", None, None),
            P("req", None, None),
            P("req", None, None),
            P("req", None, None),
            P("req", None, None),
            P("req", "exp", None, None),
        ),
        out_specs=P(("req", "exp"), None),
        check_vma=False,
    )
```

```python
import jax
import jax.numpy as jnp
from jax import lax
from jax.sharding import PartitionSpec as P
from jax.experimental import pallas as pl
from jax.experimental.pallas import tpu as pltpu

HEADS = 12
KVH = 2
HD = 128
EXPERTS = 32
WINDOW = 4096
CAP = 64


EPSILON = 1e-06
NEGATIVE = -1e30


def scaled_norm(inputs, gain):
    floats = inputs.astype(jnp.float32)
    inverse = lax.rsqrt(jnp.mean(floats * floats, axis=-1, keepdims=True) + EPSILON)
    return (floats * inverse * gain).astype(jnp.bfloat16)


def segment_of(positions, lengths):
    seg_ends = jnp.cumsum(lengths)
    return jnp.sum((positions[:, None] >= seg_ends[None, :]).astype(jnp.int32), axis=1)


def adapter_select(token_adapter, adapter_count, rank_size):
    owners = jnp.repeat(jnp.arange(adapter_count, dtype=jnp.int32), rank_size)
    return token_adapter[:, None] == owners[None, :]


def low_coords(inputs, select, joined):
    coords = jnp.dot(inputs, joined, preferred_element_type=jnp.float32)
    return jnp.where(select, coords, 0.0).astype(jnp.bfloat16)


def low_rank(inputs, select, joined, second):
    coords = low_coords(inputs, select, joined)
    return jnp.dot(coords, second, preferred_element_type=jnp.float32)


KEY_BLOCK = 512


def attention_kernel(first_ref, bmin_ref, bmax_ref, qrange_ref, q_ref, k_ref, v_ref, qseg_ref,
                     kseg_ref, init_ref, o_ref, max_ref, sum_ref, acc_ref):
    j = pl.program_id(1)
    tok_rows = qseg_ref.shape[0]
    rows = q_ref.shape[1]
    group_size = rows // tok_rows
    first_pos = first_ref[0]
    low = jnp.maximum(first_pos - (WINDOW - 1), 0) // KEY_BLOCK
    high = (first_pos + tok_rows - 1) // KEY_BLOCK

    @pl.when(j == 0)
    def _():
        max_ref[...] = init_ref[0]
        sum_ref[...] = jnp.ones_like(sum_ref)
        acc_ref[...] = jnp.zeros_like(acc_ref)

    block = jnp.minimum(low + j, high)
    seg_low = bmin_ref[block]
    seg_high = bmax_ref[block]
    shares_segment = (seg_low == 0) | (
        (seg_high >= qrange_ref[0]) & (seg_low <= qrange_ref[1])
    )

    @pl.when((low + j <= high) & shares_segment)
    def _():
        scores = lax.dot_general(
            q_ref[0], k_ref[...], (((1,), (1,)), ((), ())),
            preferred_element_type=jnp.float32,
        ) * HD ** (-0.5)
        query_pos = first_pos + lax.broadcasted_iota(jnp.int32, (tok_rows, KEY_BLOCK), 0)
        key_pos = block * KEY_BLOCK + lax.broadcasted_iota(jnp.int32, (tok_rows, KEY_BLOCK), 1)
        key_seg = kseg_ref[...]
        allowed = (
            (key_pos <= query_pos)
            & (query_pos - key_pos < WINDOW)
            & ((key_seg == qseg_ref[...]) | (key_seg == 0))
        )
        scores = jnp.where(
            allowed[None], scores.reshape(group_size, tok_rows, KEY_BLOCK), NEGATIVE
        ).reshape(rows, KEY_BLOCK)
        prev_max = max_ref[...]
        new_max = jnp.maximum(prev_max, jnp.max(scores, axis=1, keepdims=True))
        factor = jnp.exp(prev_max - new_max)
        weights = jnp.exp(scores - new_max)
        sum_ref[...] = sum_ref[...] * factor + jnp.sum(weights, axis=1, keepdims=True)
        acc_ref[...] = acc_ref[...] * factor + jnp.dot(
            weights.astype(jnp.bfloat16), v_ref[...], preferred_element_type=jnp.float32
        )
        max_ref[...] = new_max

    @pl.when(j == pl.num_programs(1) - 1)
    def _():
        o_ref[0] = (acc_ref[...] / sum_ref[...]).astype(o_ref.dtype)


def window_attention(query_cols, key_piece, positions, segments, lengths, sink_logits):
    tok_rows = query_cols.shape[0]
    group_size = HEADS // KVH
    rows = group_size * tok_rows
    piece_rows = key_piece.shape[0]
    block_total = piece_rows // KEY_BLOCK
    steps = min(block_total, (WINDOW + tok_rows - 2) // KEY_BLOCK + 2)
    queries = jnp.transpose(
        query_cols.reshape(tok_rows, KVH, group_size, HD), (1, 2, 0, 3)
    ).reshape(KVH, rows, HD)
    key_seg = segment_of(jnp.arange(piece_rows, dtype=jnp.int32), lengths).reshape(1, piece_rows)
    query_seg = segments.reshape(tok_rows, 1)
    init = jnp.broadcast_to(
        sink_logits.reshape(KVH, group_size, 1, 1), (KVH, group_size, tok_rows, 1)
    ).reshape(KVH, rows, 1)
    first = positions[:1]
    block_seg = key_seg.reshape(block_total, KEY_BLOCK)
    block_min = jnp.min(block_seg, axis=1)
    block_max = jnp.max(block_seg, axis=1)
    query_range = jnp.stack([segments[0], segments[-1]])

    def key_block(h, j, first_ref, *_):
        f = first_ref[0]
        low = jnp.maximum(f - (WINDOW - 1), 0) // KEY_BLOCK
        high = (f + tok_rows - 1) // KEY_BLOCK
        return jnp.minimum(low + j, high)

    grid_spec = pltpu.PrefetchScalarGridSpec(
        num_scalar_prefetch=4,
        grid=(KVH, steps),
        in_specs=[
            pl.BlockSpec((1, rows, HD), lambda h, j, f, *_: (h, 0, 0)),
            pl.BlockSpec((KEY_BLOCK, HD), lambda h, j, f, *_: (key_block(h, j, f), h)),
            pl.BlockSpec((KEY_BLOCK, HD), lambda h, j, f, *_: (key_block(h, j, f), KVH + h)),
            pl.BlockSpec((tok_rows, 1), lambda h, j, f, *_: (0, 0)),
            pl.BlockSpec((1, KEY_BLOCK), lambda h, j, f, *_: (0, key_block(h, j, f))),
            pl.BlockSpec((1, rows, 1), lambda h, j, f, *_: (h, 0, 0)),
        ],
        out_specs=pl.BlockSpec((1, rows, HD), lambda h, j, f, *_: (h, 0, 0)),
        scratch_shapes=[
            pltpu.VMEM((rows, 1), jnp.float32),
            pltpu.VMEM((rows, 1), jnp.float32),
            pltpu.VMEM((rows, HD), jnp.float32),
        ],
    )
    out = pl.pallas_call(
        attention_kernel,
        grid_spec=grid_spec,
        out_shape=jax.ShapeDtypeStruct((KVH, rows, HD), jnp.bfloat16),
        compiler_params=pltpu.CompilerParams(dimension_semantics=("arbitrary", "arbitrary")),
    )(first, block_min, block_max, query_range, queries, key_piece, key_piece, query_seg, key_seg, init)
    return jnp.transpose(
        out.reshape(KVH, group_size, tok_rows, HD), (2, 0, 1, 3)
    ).reshape(tok_rows, HEADS * HD)


def gather_weights(attention_in, downs, ups, expert_up, axis_name):
    inner_width = attention_in.shape[0]
    in_width = attention_in.shape[1]
    down_cols = [jnp.transpose(f, (1, 0, 2)).reshape(inner_width, -1) for f in downs]
    local_adapters, local_experts, rank_size, hidden_width = expert_up.shape
    up_rows = [f.reshape(-1, f.shape[2]) for f in ups] + [
        jnp.transpose(expert_up, (0, 2, 1, 3)).reshape(local_adapters * rank_size, -1)
    ]
    wide = lax.all_gather(
        jnp.concatenate([attention_in] + down_cols, axis=1), axis_name, axis=1, tiled=True
    )
    peers = wide.shape[1] // (in_width + sum(c.shape[1] for c in down_cols))
    wide = wide.reshape(inner_width, peers, -1)
    full_in = wide[:, :, :in_width].reshape(inner_width, -1)
    joined = []
    offset = in_width
    for c in down_cols:
        joined.append(wide[:, :, offset : offset + c.shape[1]].reshape(inner_width, -1))
        offset += c.shape[1]
    tall = lax.all_gather(jnp.concatenate(up_rows, axis=1), axis_name, axis=0, tiled=True)
    seconds = []
    offset = 0
    for r in up_rows:
        seconds.append(tall[:, offset : offset + r.shape[1]])
        offset += r.shape[1]
    bank = jnp.transpose(
        seconds[-1].reshape(tall.shape[0], local_experts, hidden_width), (1, 0, 2)
    )
    return full_in, joined, seconds[:-1], bank


def body(
    tokens,
    segment_lengths,
    segment_adapters,
    routes,
    gate_weights,
    attention_gain,
    attention_in,
    sink_logits,
    attention_out,
    expert_gain,
    expert_gate_up,
    expert_down,
    adapter_in_down,
    adapter_in_up,
    adapter_out_down,
    adapter_out_up,
    adapter_expert_down,
    adapter_expert_up,
):
    tok_rows = tokens.shape[0]
    lengths = segment_lengths[0]
    segment_total = lengths.shape[0]
    first_pos = lax.axis_index("exp") * tok_rows
    positions = first_pos + jnp.arange(tok_rows, dtype=jnp.int32)
    segments = segment_of(positions, lengths)
    matches = segments[:, None] == jnp.arange(segment_total, dtype=jnp.int32)[None, :]
    token_adapter = jnp.sum(jnp.where(matches, segment_adapters[0][None, :], 0), axis=1)
    adapter_count = adapter_in_down.shape[0] * lax.axis_size("req")
    rank_size = adapter_in_down.shape[2]
    select = adapter_select(token_adapter, adapter_count, rank_size)
    normed = scaled_norm(tokens, attention_gain)
    full_in, joined, seconds, adapter_bank = gather_weights(
        attention_in,
        (adapter_in_down, adapter_out_down, adapter_expert_down),
        (adapter_in_up, adapter_out_up),
        adapter_expert_up,
        "req",
    )
    in_low, out_low, expert_low = joined
    in_high, out_high = seconds
    full_out = lax.all_gather(attention_out, "req", axis=1, tiled=True)
    base_heads = jnp.dot(normed, full_in, preferred_element_type=jnp.float32)
    projected = (base_heads + low_rank(normed, select, in_low, in_high)).astype(jnp.bfloat16)
    group_size = HEADS // KVH
    key_value = projected[:, HEADS * HD :]
    key_piece = lax.all_gather(key_value, "exp", axis=0, tiled=True)
    attended = window_attention(
        projected[:, : HEADS * HD], key_piece, positions, segments, lengths, sink_logits
    )
    base_out = jnp.dot(attended, full_out, preferred_element_type=jnp.float32)
    residual = (
        tokens.astype(jnp.float32) + base_out + low_rank(attended, select, out_low, out_high)
    ).astype(jnp.bfloat16)
    normed_two = scaled_norm(residual, expert_gain)
    low_parts = low_coords(normed_two, select, expert_low)
    top_count = routes.shape[1]
    picked = routes.reshape(-1)
    expert_hot = (picked[:, None] == jnp.arange(EXPERTS, dtype=jnp.int32)[None, :]).astype(
        jnp.int32
    )
    arrival = jnp.sum((jnp.cumsum(expert_hot, axis=0) - 1) * expert_hot, axis=1)
    slot_index = picked * CAP + arrival
    slot_count = EXPERTS * CAP
    slot_ids = jnp.arange(slot_count, dtype=jnp.int32)
    token_slots = slot_index.reshape(tok_rows, top_count)
    dispatch = jnp.any(
        token_slots[None, :, :] == slot_ids[:, None, None], axis=2
    ).astype(jnp.bfloat16)
    peer_count = lax.axis_size("exp")
    local_experts = EXPERTS // peer_count
    row_width = normed_two.shape[1]
    send = jnp.dot(
        dispatch,
        jnp.concatenate([normed_two, low_parts], axis=1),
        preferred_element_type=jnp.float32,
    ).astype(jnp.bfloat16).reshape(peer_count, local_experts, CAP, -1)
    hidden_width = expert_down.shape[1]

    def expert_chunk(chunk):
        arrived = lax.all_to_all(chunk, "exp", split_axis=0, concat_axis=0, tiled=True)
        arrived_rows = arrived[..., :row_width]
        arrived_low = arrived[..., row_width:]
        gate_up = jnp.einsum(
            "necd,edf->necf", arrived_rows, expert_gate_up, preferred_element_type=jnp.float32
        )
        up_part = gate_up[..., hidden_width:] + jnp.einsum(
            "necr,erf->necf", arrived_low, adapter_bank, preferred_element_type=jnp.float32
        )
        hidden = (jax.nn.relu(gate_up[..., :hidden_width]) * up_part).astype(jnp.bfloat16)
        outputs = jnp.einsum(
            "necf,efd->necd", hidden, expert_down, preferred_element_type=jnp.float32
        ).astype(jnp.bfloat16)
        return lax.all_to_all(outputs, "exp", split_axis=0, concat_axis=0, tiled=True)

    chunk_count = 4
    part = CAP // chunk_count
    returned = jnp.concatenate(
        [expert_chunk(send[:, :, c * part : (c + 1) * part]) for c in range(chunk_count)], axis=2
    )
    flat_back = returned.reshape(EXPERTS * CAP, -1)
    gate_grid = jnp.sum(
        jnp.where(
            token_slots[:, :, None] == slot_ids[None, None, :], gate_weights[:, :, None], 0.0
        ),
        axis=1,
    )
    gate_high = gate_grid.astype(jnp.bfloat16)
    gate_low = (gate_grid - gate_high.astype(jnp.float32)).astype(jnp.bfloat16)
    combined = jnp.dot(gate_high, flat_back, preferred_element_type=jnp.float32) + jnp.dot(
        gate_low, flat_back, preferred_element_type=jnp.float32
    )
    return (residual.astype(jnp.float32) + combined).astype(jnp.bfloat16)


def solution(mesh):
    return jax.shard_map(
        body,
        mesh=mesh,
        in_specs=(
            P(("req", "exp"), None),
            P("req", None),
            P("req", None),
            P(("req", "exp"), None),
            P(("req", "exp"), None),
            P(),
            P(None, "req"),
            P(),
            P(None, "req"),
            P(),
            P("exp", None, None),
            P("exp", None, None),
            P("req", None, None),
            P("req", None, None),
            P("req", None, None),
            P("req", None, None),
            P("req", None, None),
            P("req", "exp", None, None),
        ),
        out_specs=P(("req", "exp"), None),
        check_vma=False,
    )
```

```python
import jax
import jax.numpy as jnp
from jax import lax
from jax.sharding import PartitionSpec as P
from jax.experimental import pallas as pl
from jax.experimental.pallas import tpu as pltpu

HEADS = 12
KVH = 2
HD = 128
EXPERTS = 32
WINDOW = 4096
CAP = 64


EPSILON = 1e-06
NEGATIVE = -1e30


def scaled_norm(inputs, gain):
    floats = inputs.astype(jnp.float32)
    inverse = lax.rsqrt(jnp.mean(floats * floats, axis=-1, keepdims=True) + EPSILON)
    return (floats * inverse * gain).astype(jnp.bfloat16)


def segment_of(positions, lengths):
    seg_ends = jnp.cumsum(lengths)
    return jnp.sum((positions[:, None] >= seg_ends[None, :]).astype(jnp.int32), axis=1)


def adapter_select(token_adapter, adapter_count, rank_size):
    owners = jnp.repeat(jnp.arange(adapter_count, dtype=jnp.int32), rank_size)
    return token_adapter[:, None] == owners[None, :]


def low_coords(inputs, select, joined):
    coords = jnp.dot(inputs, joined, preferred_element_type=jnp.float32)
    return jnp.where(select, coords, 0.0).astype(jnp.bfloat16)


def low_rank(inputs, select, joined, second):
    coords = low_coords(inputs, select, joined)
    return jnp.dot(coords, second, preferred_element_type=jnp.float32)


KEY_BLOCK = 512


def attention_kernel(first_ref, bmin_ref, bmax_ref, qrange_ref, q_ref, k_ref, v_ref, qseg_ref,
                     kseg_ref, init_ref, o_ref, max_ref, sum_ref, acc_ref):
    j = pl.program_id(1)
    tok_rows = qseg_ref.shape[0]
    rows = q_ref.shape[1]
    group_size = rows // tok_rows
    first_pos = first_ref[0]
    low = jnp.maximum(first_pos - (WINDOW - 1), 0) // KEY_BLOCK
    high = (first_pos + tok_rows - 1) // KEY_BLOCK

    @pl.when(j == 0)
    def _():
        max_ref[...] = init_ref[0]
        sum_ref[...] = jnp.ones_like(sum_ref)
        acc_ref[...] = jnp.zeros_like(acc_ref)

    block = jnp.minimum(low + j, high)
    seg_low = bmin_ref[block]
    seg_high = bmax_ref[block]
    shares_segment = (seg_low == 0) | (
        (seg_high >= qrange_ref[0]) & (seg_low <= qrange_ref[1])
    )

    @pl.when((low + j <= high) & shares_segment)
    def _():
        scores = lax.dot_general(
            q_ref[0], k_ref[...], (((1,), (1,)), ((), ())),
            preferred_element_type=jnp.float32,
        ) * HD ** (-0.5)
        query_pos = first_pos + lax.broadcasted_iota(jnp.int32, (tok_rows, KEY_BLOCK), 0)
        key_pos = block * KEY_BLOCK + lax.broadcasted_iota(jnp.int32, (tok_rows, KEY_BLOCK), 1)
        key_seg = kseg_ref[...]
        allowed = (
            (key_pos <= query_pos)
            & (query_pos - key_pos < WINDOW)
            & ((key_seg == qseg_ref[...]) | (key_seg == 0))
        )
        scores = jnp.where(
            allowed[None], scores.reshape(group_size, tok_rows, KEY_BLOCK), NEGATIVE
        ).reshape(rows, KEY_BLOCK)
        prev_max = max_ref[...]
        new_max = jnp.maximum(prev_max, jnp.max(scores, axis=1, keepdims=True))
        factor = jnp.exp(prev_max - new_max)
        weights = jnp.exp(scores - new_max)
        sum_ref[...] = sum_ref[...] * factor + jnp.sum(weights, axis=1, keepdims=True)
        acc_ref[...] = acc_ref[...] * factor + jnp.dot(
            weights.astype(jnp.bfloat16), v_ref[...], preferred_element_type=jnp.float32
        )
        max_ref[...] = new_max

    @pl.when(j == pl.num_programs(1) - 1)
    def _():
        o_ref[0] = (acc_ref[...] / sum_ref[...]).astype(o_ref.dtype)


def window_attention(query_cols, key_piece, positions, segments, lengths, sink_logits):
    tok_rows = query_cols.shape[0]
    group_size = HEADS // KVH
    rows = group_size * tok_rows
    piece_rows = key_piece.shape[0]
    block_total = piece_rows // KEY_BLOCK
    steps = min(block_total, (WINDOW + tok_rows - 2) // KEY_BLOCK + 2)
    queries = jnp.transpose(
        query_cols.reshape(tok_rows, KVH, group_size, HD), (1, 2, 0, 3)
    ).reshape(KVH, rows, HD)
    key_seg = segment_of(jnp.arange(piece_rows, dtype=jnp.int32), lengths).reshape(1, piece_rows)
    query_seg = segments.reshape(tok_rows, 1)
    init = jnp.broadcast_to(
        sink_logits.reshape(KVH, group_size, 1, 1), (KVH, group_size, tok_rows, 1)
    ).reshape(KVH, rows, 1)
    first = positions[:1]
    block_seg = key_seg.reshape(block_total, KEY_BLOCK)
    block_min = jnp.min(block_seg, axis=1)
    block_max = jnp.max(block_seg, axis=1)
    query_range = jnp.stack([segments[0], segments[-1]])

    def key_block(h, j, first_ref, *_):
        f = first_ref[0]
        low = jnp.maximum(f - (WINDOW - 1), 0) // KEY_BLOCK
        high = (f + tok_rows - 1) // KEY_BLOCK
        return jnp.minimum(low + j, high)

    grid_spec = pltpu.PrefetchScalarGridSpec(
        num_scalar_prefetch=4,
        grid=(KVH, steps),
        in_specs=[
            pl.BlockSpec((1, rows, HD), lambda h, j, f, *_: (h, 0, 0)),
            pl.BlockSpec((KEY_BLOCK, HD), lambda h, j, f, *_: (key_block(h, j, f), h)),
            pl.BlockSpec((KEY_BLOCK, HD), lambda h, j, f, *_: (key_block(h, j, f), KVH + h)),
            pl.BlockSpec((tok_rows, 1), lambda h, j, f, *_: (0, 0)),
            pl.BlockSpec((1, KEY_BLOCK), lambda h, j, f, *_: (0, key_block(h, j, f))),
            pl.BlockSpec((1, rows, 1), lambda h, j, f, *_: (h, 0, 0)),
        ],
        out_specs=pl.BlockSpec((1, rows, HD), lambda h, j, f, *_: (h, 0, 0)),
        scratch_shapes=[
            pltpu.VMEM((rows, 1), jnp.float32),
            pltpu.VMEM((rows, 1), jnp.float32),
            pltpu.VMEM((rows, HD), jnp.float32),
        ],
    )
    out = pl.pallas_call(
        attention_kernel,
        grid_spec=grid_spec,
        out_shape=jax.ShapeDtypeStruct((KVH, rows, HD), jnp.bfloat16),
        compiler_params=pltpu.CompilerParams(dimension_semantics=("arbitrary", "arbitrary")),
    )(first, block_min, block_max, query_range, queries, key_piece, key_piece, query_seg, key_seg, init)
    return jnp.transpose(
        out.reshape(KVH, group_size, tok_rows, HD), (2, 0, 1, 3)
    ).reshape(tok_rows, HEADS * HD)


def gather_weights(attention_in, downs, ups, expert_up, axis_name):
    inner_width = attention_in.shape[0]
    in_width = attention_in.shape[1]
    down_cols = [jnp.transpose(f, (1, 0, 2)).reshape(inner_width, -1) for f in downs]
    local_adapters, local_experts, rank_size, hidden_width = expert_up.shape
    up_rows = [f.reshape(-1, f.shape[2]) for f in ups] + [
        jnp.transpose(expert_up, (0, 2, 1, 3)).reshape(local_adapters * rank_size, -1)
    ]
    wide = lax.all_gather(
        jnp.concatenate([attention_in] + down_cols, axis=1), axis_name, axis=1, tiled=True
    )
    peers = wide.shape[1] // (in_width + sum(c.shape[1] for c in down_cols))
    wide = wide.reshape(inner_width, peers, -1)
    full_in = wide[:, :, :in_width].reshape(inner_width, -1)
    joined = []
    offset = in_width
    for c in down_cols:
        joined.append(wide[:, :, offset : offset + c.shape[1]].reshape(inner_width, -1))
        offset += c.shape[1]
    tall = lax.all_gather(jnp.concatenate(up_rows, axis=1), axis_name, axis=0, tiled=True)
    seconds = []
    offset = 0
    for r in up_rows:
        seconds.append(tall[:, offset : offset + r.shape[1]])
        offset += r.shape[1]
    bank = jnp.transpose(
        seconds[-1].reshape(tall.shape[0], local_experts, hidden_width), (1, 0, 2)
    )
    return full_in, joined, seconds[:-1], bank


def body(
    tokens,
    segment_lengths,
    segment_adapters,
    routes,
    gate_weights,
    attention_gain,
    attention_in,
    sink_logits,
    attention_out,
    expert_gain,
    expert_gate_up,
    expert_down,
    adapter_in_down,
    adapter_in_up,
    adapter_out_down,
    adapter_out_up,
    adapter_expert_down,
    adapter_expert_up,
):
    tok_rows = tokens.shape[0]
    lengths = segment_lengths[0]
    segment_total = lengths.shape[0]
    first_pos = lax.axis_index("exp") * tok_rows
    positions = first_pos + jnp.arange(tok_rows, dtype=jnp.int32)
    segments = segment_of(positions, lengths)
    matches = segments[:, None] == jnp.arange(segment_total, dtype=jnp.int32)[None, :]
    token_adapter = jnp.sum(jnp.where(matches, segment_adapters[0][None, :], 0), axis=1)
    adapter_count = adapter_in_down.shape[0] * lax.axis_size("req")
    rank_size = adapter_in_down.shape[2]
    select = adapter_select(token_adapter, adapter_count, rank_size)
    normed = scaled_norm(tokens, attention_gain)
    full_in, joined, seconds, adapter_bank = gather_weights(
        attention_in,
        (adapter_in_down, adapter_out_down, adapter_expert_down),
        (adapter_in_up, adapter_out_up),
        adapter_expert_up,
        "req",
    )
    in_low, out_low, expert_low = joined
    in_high, out_high = seconds
    full_out = lax.all_gather(attention_out, "req", axis=1, tiled=True)
    base_heads = jnp.dot(normed, full_in, preferred_element_type=jnp.float32)
    projected = (base_heads + low_rank(normed, select, in_low, in_high)).astype(jnp.bfloat16)
    group_size = HEADS // KVH
    key_value = projected[:, HEADS * HD :]
    key_piece = lax.all_gather(key_value, "exp", axis=0, tiled=True)
    attended = window_attention(
        projected[:, : HEADS * HD], key_piece, positions, segments, lengths, sink_logits
    )
    base_out = jnp.dot(attended, full_out, preferred_element_type=jnp.float32)
    residual = (
        tokens.astype(jnp.float32) + base_out + low_rank(attended, select, out_low, out_high)
    ).astype(jnp.bfloat16)
    normed_two = scaled_norm(residual, expert_gain)
    low_parts = low_coords(normed_two, select, expert_low)
    top_count = routes.shape[1]
    picked = routes.reshape(-1)
    expert_hot = (picked[:, None] == jnp.arange(EXPERTS, dtype=jnp.int32)[None, :]).astype(
        jnp.int32
    )
    arrival = jnp.sum((jnp.cumsum(expert_hot, axis=0) - 1) * expert_hot, axis=1)
    slot_index = picked * CAP + arrival
    slot_count = EXPERTS * CAP
    slot_ids = jnp.arange(slot_count, dtype=jnp.int32)
    token_slots = slot_index.reshape(tok_rows, top_count)
    dispatch = jnp.any(
        token_slots[None, :, :] == slot_ids[:, None, None], axis=2
    ).astype(jnp.bfloat16)
    peer_count = lax.axis_size("exp")
    local_experts = EXPERTS // peer_count
    row_width = normed_two.shape[1]
    low_compact = jnp.sum(
        low_parts.reshape(tok_rows, adapter_count, rank_size).astype(jnp.float32), axis=1
    ).astype(jnp.bfloat16)
    lane_pad = 128 - rank_size - 1
    payload = jnp.concatenate(
        [
            normed_two,
            low_compact,
            token_adapter.astype(jnp.bfloat16)[:, None],
            jnp.zeros((tok_rows, lane_pad), jnp.bfloat16),
        ],
        axis=1,
    )
    send = jnp.dot(
        dispatch,
        payload,
        preferred_element_type=jnp.float32,
    ).astype(jnp.bfloat16).reshape(peer_count, local_experts, CAP, -1)
    hidden_width = expert_down.shape[1]

    def expert_chunk(chunk):
        arrived = lax.all_to_all(chunk, "exp", split_axis=0, concat_axis=0, tiled=True)
        arrived_rows = arrived[..., :row_width]
        owner = arrived[..., row_width + rank_size : row_width + rank_size + 1]
        arrived_low = jnp.where(
            owner[..., None] == jnp.arange(adapter_count, dtype=jnp.int32)[:, None].astype(owner.dtype),
            arrived[..., None, row_width : row_width + rank_size],
            0,
        ).reshape(arrived.shape[:-1] + (adapter_count * rank_size,))
        gate_up = jnp.einsum(
            "necd,edf->necf", arrived_rows, expert_gate_up, preferred_element_type=jnp.float32
        )
        up_part = gate_up[..., hidden_width:] + jnp.einsum(
            "necr,erf->necf", arrived_low, adapter_bank, preferred_element_type=jnp.float32
        )
        hidden = (jax.nn.relu(gate_up[..., :hidden_width]) * up_part).astype(jnp.bfloat16)
        outputs = jnp.einsum(
            "necf,efd->necd", hidden, expert_down, preferred_element_type=jnp.float32
        ).astype(jnp.bfloat16)
        return lax.all_to_all(outputs, "exp", split_axis=0, concat_axis=0, tiled=True)

    half = CAP // 2
    returned = jnp.concatenate(
        [expert_chunk(send[:, :, :half]), expert_chunk(send[:, :, half:])], axis=2
    )
    flat_back = returned.reshape(EXPERTS * CAP, -1)
    gate_grid = jnp.sum(
        jnp.where(
            token_slots[:, :, None] == slot_ids[None, None, :], gate_weights[:, :, None], 0.0
        ),
        axis=1,
    )
    gate_high = gate_grid.astype(jnp.bfloat16)
    gate_low = (gate_grid - gate_high.astype(jnp.float32)).astype(jnp.bfloat16)
    combined = jnp.dot(gate_high, flat_back, preferred_element_type=jnp.float32) + jnp.dot(
        gate_low, flat_back, preferred_element_type=jnp.float32
    )
    return (residual.astype(jnp.float32) + combined).astype(jnp.bfloat16)


def solution(mesh):
    return jax.shard_map(
        body,
        mesh=mesh,
        in_specs=(
            P(("req", "exp"), None),
            P("req", None),
            P("req", None),
            P(("req", "exp"), None),
            P(("req", "exp"), None),
            P(),
            P(None, "req"),
            P(),
            P(None, "req"),
            P(),
            P("exp", None, None),
            P("exp", None, None),
            P("req", None, None),
            P("req", None, None),
            P("req", None, None),
            P("req", None, None),
            P("req", None, None),
            P("req", "exp", None, None),
        ),
        out_specs=P(("req", "exp"), None),
        check_vma=False,
    )
```

```python
import jax
import jax.numpy as jnp
from jax import lax
from jax.sharding import PartitionSpec as P
from jax.experimental import pallas as pl
from jax.experimental.pallas import tpu as pltpu

HEADS = 12
KVH = 2
HD = 128
EXPERTS = 32
WINDOW = 4096
CAP = 64


EPSILON = 1e-06
NEGATIVE = -1e30


def scaled_norm(inputs, gain):
    floats = inputs.astype(jnp.float32)
    inverse = lax.rsqrt(jnp.mean(floats * floats, axis=-1, keepdims=True) + EPSILON)
    return (floats * inverse * gain).astype(jnp.bfloat16)


def segment_of(positions, lengths):
    seg_ends = jnp.cumsum(lengths)
    return jnp.sum((positions[:, None] >= seg_ends[None, :]).astype(jnp.int32), axis=1)


def adapter_select(token_adapter, adapter_count, rank_size):
    owners = jnp.repeat(jnp.arange(adapter_count, dtype=jnp.int32), rank_size)
    return token_adapter[:, None] == owners[None, :]


def low_coords(inputs, select, joined):
    coords = jnp.dot(inputs, joined, preferred_element_type=jnp.float32)
    return jnp.where(select, coords, 0.0).astype(jnp.bfloat16)


def low_rank(inputs, select, joined, second):
    coords = low_coords(inputs, select, joined)
    return jnp.dot(coords, second, preferred_element_type=jnp.float32)


KEY_BLOCK = 256


def attention_kernel(first_ref, bmin_ref, bmax_ref, qrange_ref, q_ref, k_ref, v_ref, qseg_ref,
                     kseg_ref, init_ref, o_ref, max_ref, sum_ref, acc_ref):
    j = pl.program_id(1)
    tok_rows = qseg_ref.shape[0]
    rows = q_ref.shape[1]
    group_size = rows // tok_rows
    first_pos = first_ref[0]
    low = jnp.maximum(first_pos - (WINDOW - 1), 0) // KEY_BLOCK
    high = (first_pos + tok_rows - 1) // KEY_BLOCK

    @pl.when(j == 0)
    def _():
        max_ref[...] = init_ref[0]
        sum_ref[...] = jnp.ones_like(sum_ref)
        acc_ref[...] = jnp.zeros_like(acc_ref)

    block = jnp.minimum(low + j, high)
    seg_low = bmin_ref[block]
    seg_high = bmax_ref[block]
    shares_segment = (seg_low == 0) | (
        (seg_high >= qrange_ref[0]) & (seg_low <= qrange_ref[1])
    )

    @pl.when((low + j <= high) & shares_segment)
    def _():
        scores = lax.dot_general(
            q_ref[0], k_ref[...], (((1,), (1,)), ((), ())),
            preferred_element_type=jnp.float32,
        ) * HD ** (-0.5)
        query_pos = first_pos + lax.broadcasted_iota(jnp.int32, (tok_rows, KEY_BLOCK), 0)
        key_pos = block * KEY_BLOCK + lax.broadcasted_iota(jnp.int32, (tok_rows, KEY_BLOCK), 1)
        key_seg = kseg_ref[...]
        allowed = (
            (key_pos <= query_pos)
            & (query_pos - key_pos < WINDOW)
            & ((key_seg == qseg_ref[...]) | (key_seg == 0))
        )
        scores = jnp.where(
            allowed[None], scores.reshape(group_size, tok_rows, KEY_BLOCK), NEGATIVE
        ).reshape(rows, KEY_BLOCK)
        prev_max = max_ref[...]
        new_max = jnp.maximum(prev_max, jnp.max(scores, axis=1, keepdims=True))
        factor = jnp.exp(prev_max - new_max)
        weights = jnp.exp(scores - new_max)
        sum_ref[...] = sum_ref[...] * factor + jnp.sum(weights, axis=1, keepdims=True)
        acc_ref[...] = acc_ref[...] * factor + jnp.dot(
            weights.astype(jnp.bfloat16), v_ref[...], preferred_element_type=jnp.float32
        )
        max_ref[...] = new_max

    @pl.when(j == pl.num_programs(1) - 1)
    def _():
        o_ref[0] = (acc_ref[...] / sum_ref[...]).astype(o_ref.dtype)


def window_attention(query_cols, key_piece, positions, segments, lengths, sink_logits):
    tok_rows = query_cols.shape[0]
    group_size = HEADS // KVH
    rows = group_size * tok_rows
    piece_rows = key_piece.shape[0]
    block_total = piece_rows // KEY_BLOCK
    steps = min(block_total, (WINDOW + tok_rows - 2) // KEY_BLOCK + 2)
    queries = jnp.transpose(
        query_cols.reshape(tok_rows, KVH, group_size, HD), (1, 2, 0, 3)
    ).reshape(KVH, rows, HD)
    key_seg = segment_of(jnp.arange(piece_rows, dtype=jnp.int32), lengths).reshape(1, piece_rows)
    query_seg = segments.reshape(tok_rows, 1)
    init = jnp.broadcast_to(
        sink_logits.reshape(KVH, group_size, 1, 1), (KVH, group_size, tok_rows, 1)
    ).reshape(KVH, rows, 1)
    first = positions[:1]
    block_seg = key_seg.reshape(block_total, KEY_BLOCK)
    block_min = jnp.min(block_seg, axis=1)
    block_max = jnp.max(block_seg, axis=1)
    query_range = jnp.stack([segments[0], segments[-1]])

    def key_block(h, j, first_ref, *_):
        f = first_ref[0]
        low = jnp.maximum(f - (WINDOW - 1), 0) // KEY_BLOCK
        high = (f + tok_rows - 1) // KEY_BLOCK
        return jnp.minimum(low + j, high)

    grid_spec = pltpu.PrefetchScalarGridSpec(
        num_scalar_prefetch=4,
        grid=(KVH, steps),
        in_specs=[
            pl.BlockSpec((1, rows, HD), lambda h, j, f, *_: (h, 0, 0)),
            pl.BlockSpec((KEY_BLOCK, HD), lambda h, j, f, *_: (key_block(h, j, f), h)),
            pl.BlockSpec((KEY_BLOCK, HD), lambda h, j, f, *_: (key_block(h, j, f), KVH + h)),
            pl.BlockSpec((tok_rows, 1), lambda h, j, f, *_: (0, 0)),
            pl.BlockSpec((1, KEY_BLOCK), lambda h, j, f, *_: (0, key_block(h, j, f))),
            pl.BlockSpec((1, rows, 1), lambda h, j, f, *_: (h, 0, 0)),
        ],
        out_specs=pl.BlockSpec((1, rows, HD), lambda h, j, f, *_: (h, 0, 0)),
        scratch_shapes=[
            pltpu.VMEM((rows, 1), jnp.float32),
            pltpu.VMEM((rows, 1), jnp.float32),
            pltpu.VMEM((rows, HD), jnp.float32),
        ],
    )
    out = pl.pallas_call(
        attention_kernel,
        grid_spec=grid_spec,
        out_shape=jax.ShapeDtypeStruct((KVH, rows, HD), jnp.bfloat16),
        compiler_params=pltpu.CompilerParams(dimension_semantics=("arbitrary", "arbitrary")),
    )(first, block_min, block_max, query_range, queries, key_piece, key_piece, query_seg, key_seg, init)
    return jnp.transpose(
        out.reshape(KVH, group_size, tok_rows, HD), (2, 0, 1, 3)
    ).reshape(tok_rows, HEADS * HD)


def gather_weights(attention_in, downs, ups, expert_up, axis_name):
    inner_width = attention_in.shape[0]
    in_width = attention_in.shape[1]
    down_cols = [jnp.transpose(f, (1, 0, 2)).reshape(inner_width, -1) for f in downs]
    local_adapters, local_experts, rank_size, hidden_width = expert_up.shape
    up_rows = [f.reshape(-1, f.shape[2]) for f in ups] + [
        jnp.transpose(expert_up, (0, 2, 1, 3)).reshape(local_adapters * rank_size, -1)
    ]
    wide = lax.all_gather(
        jnp.concatenate([attention_in] + down_cols, axis=1), axis_name, axis=1, tiled=True
    )
    peers = wide.shape[1] // (in_width + sum(c.shape[1] for c in down_cols))
    wide = wide.reshape(inner_width, peers, -1)
    full_in = wide[:, :, :in_width].reshape(inner_width, -1)
    joined = []
    offset = in_width
    for c in down_cols:
        joined.append(wide[:, :, offset : offset + c.shape[1]].reshape(inner_width, -1))
        offset += c.shape[1]
    tall = lax.all_gather(jnp.concatenate(up_rows, axis=1), axis_name, axis=0, tiled=True)
    seconds = []
    offset = 0
    for r in up_rows:
        seconds.append(tall[:, offset : offset + r.shape[1]])
        offset += r.shape[1]
    bank = jnp.transpose(
        seconds[-1].reshape(tall.shape[0], local_experts, hidden_width), (1, 0, 2)
    )
    return full_in, joined, seconds[:-1], bank


def body(
    tokens,
    segment_lengths,
    segment_adapters,
    routes,
    gate_weights,
    attention_gain,
    attention_in,
    sink_logits,
    attention_out,
    expert_gain,
    expert_gate_up,
    expert_down,
    adapter_in_down,
    adapter_in_up,
    adapter_out_down,
    adapter_out_up,
    adapter_expert_down,
    adapter_expert_up,
):
    tok_rows = tokens.shape[0]
    lengths = segment_lengths[0]
    segment_total = lengths.shape[0]
    first_pos = lax.axis_index("exp") * tok_rows
    positions = first_pos + jnp.arange(tok_rows, dtype=jnp.int32)
    segments = segment_of(positions, lengths)
    matches = segments[:, None] == jnp.arange(segment_total, dtype=jnp.int32)[None, :]
    token_adapter = jnp.sum(jnp.where(matches, segment_adapters[0][None, :], 0), axis=1)
    adapter_count = adapter_in_down.shape[0] * lax.axis_size("req")
    rank_size = adapter_in_down.shape[2]
    select = adapter_select(token_adapter, adapter_count, rank_size)
    normed = scaled_norm(tokens, attention_gain)
    full_in, joined, seconds, adapter_bank = gather_weights(
        attention_in,
        (adapter_in_down, adapter_out_down, adapter_expert_down),
        (adapter_in_up, adapter_out_up),
        adapter_expert_up,
        "req",
    )
    in_low, out_low, expert_low = joined
    in_high, out_high = seconds
    full_out = lax.all_gather(attention_out, "req", axis=1, tiled=True)
    base_heads = jnp.dot(normed, full_in, preferred_element_type=jnp.float32)
    projected = (base_heads + low_rank(normed, select, in_low, in_high)).astype(jnp.bfloat16)
    group_size = HEADS // KVH
    key_value = projected[:, HEADS * HD :]
    key_piece = lax.all_gather(key_value, "exp", axis=0, tiled=True)
    attended = window_attention(
        projected[:, : HEADS * HD], key_piece, positions, segments, lengths, sink_logits
    )
    base_out = jnp.dot(attended, full_out, preferred_element_type=jnp.float32)
    residual = (
        tokens.astype(jnp.float32) + base_out + low_rank(attended, select, out_low, out_high)
    ).astype(jnp.bfloat16)
    normed_two = scaled_norm(residual, expert_gain)
    low_parts = low_coords(normed_two, select, expert_low)
    top_count = routes.shape[1]
    picked = routes.reshape(-1)
    expert_hot = (picked[:, None] == jnp.arange(EXPERTS, dtype=jnp.int32)[None, :]).astype(
        jnp.int32
    )
    arrival = jnp.sum((jnp.cumsum(expert_hot, axis=0) - 1) * expert_hot, axis=1)
    slot_index = picked * CAP + arrival
    slot_count = EXPERTS * CAP
    slot_ids = jnp.arange(slot_count, dtype=jnp.int32)
    token_slots = slot_index.reshape(tok_rows, top_count)
    dispatch = jnp.any(
        token_slots[None, :, :] == slot_ids[:, None, None], axis=2
    ).astype(jnp.bfloat16)
    peer_count = lax.axis_size("exp")
    local_experts = EXPERTS // peer_count
    row_width = normed_two.shape[1]
    send = jnp.dot(
        dispatch,
        jnp.concatenate([normed_two, low_parts], axis=1),
        preferred_element_type=jnp.float32,
    ).astype(jnp.bfloat16).reshape(peer_count, local_experts, CAP, -1)
    hidden_width = expert_down.shape[1]

    def expert_chunk(chunk):
        arrived = lax.all_to_all(chunk, "exp", split_axis=0, concat_axis=0, tiled=True)
        arrived_rows = arrived[..., :row_width]
        arrived_low = arrived[..., row_width:]
        gate_up = jnp.einsum(
            "necd,edf->necf", arrived_rows, expert_gate_up, preferred_element_type=jnp.float32
        )
        up_part = gate_up[..., hidden_width:] + jnp.einsum(
            "necr,erf->necf", arrived_low, adapter_bank, preferred_element_type=jnp.float32
        )
        hidden = (jax.nn.relu(gate_up[..., :hidden_width]) * up_part).astype(jnp.bfloat16)
        outputs = jnp.einsum(
            "necf,efd->necd", hidden, expert_down, preferred_element_type=jnp.float32
        ).astype(jnp.bfloat16)
        return lax.all_to_all(outputs, "exp", split_axis=0, concat_axis=0, tiled=True)

    half = CAP // 2
    returned = jnp.concatenate(
        [expert_chunk(send[:, :, :half]), expert_chunk(send[:, :, half:])], axis=2
    )
    flat_back = returned.reshape(EXPERTS * CAP, -1)
    gate_grid = jnp.sum(
        jnp.where(
            token_slots[:, :, None] == slot_ids[None, None, :], gate_weights[:, :, None], 0.0
        ),
        axis=1,
    )
    gate_high = gate_grid.astype(jnp.bfloat16)
    gate_low = (gate_grid - gate_high.astype(jnp.float32)).astype(jnp.bfloat16)
    combined = jnp.dot(gate_high, flat_back, preferred_element_type=jnp.float32) + jnp.dot(
        gate_low, flat_back, preferred_element_type=jnp.float32
    )
    return (residual.astype(jnp.float32) + combined).astype(jnp.bfloat16)


def solution(mesh):
    return jax.shard_map(
        body,
        mesh=mesh,
        in_specs=(
            P(("req", "exp"), None),
            P("req", None),
            P("req", None),
            P(("req", "exp"), None),
            P(("req", "exp"), None),
            P(),
            P(None, "req"),
            P(),
            P(None, "req"),
            P(),
            P("exp", None, None),
            P("exp", None, None),
            P("req", None, None),
            P("req", None, None),
            P("req", None, None),
            P("req", None, None),
            P("req", None, None),
            P("req", "exp", None, None),
        ),
        out_specs=P(("req", "exp"), None),
        check_vma=False,
    )
```

```python
import jax
import jax.numpy as jnp
from jax import lax
from jax.sharding import PartitionSpec as P
from jax.experimental import pallas as pl
from jax.experimental.pallas import tpu as pltpu

HEADS = 12
KVH = 2
HD = 128
EXPERTS = 32
WINDOW = 4096
CAP = 64


EPSILON = 1e-06
NEGATIVE = -1e30


def scaled_norm(inputs, gain):
    floats = inputs.astype(jnp.float32)
    inverse = lax.rsqrt(jnp.mean(floats * floats, axis=-1, keepdims=True) + EPSILON)
    return (floats * inverse * gain).astype(jnp.bfloat16)


def segment_of(positions, lengths):
    seg_ends = jnp.cumsum(lengths)
    return jnp.sum((positions[:, None] >= seg_ends[None, :]).astype(jnp.int32), axis=1)


def adapter_select(token_adapter, adapter_count, rank_size):
    owners = jnp.repeat(jnp.arange(adapter_count, dtype=jnp.int32), rank_size)
    return token_adapter[:, None] == owners[None, :]


def low_coords(inputs, select, joined):
    coords = jnp.dot(inputs, joined, preferred_element_type=jnp.float32)
    return jnp.where(select, coords, 0.0).astype(jnp.bfloat16)


def low_rank(inputs, select, joined, second):
    coords = low_coords(inputs, select, joined)
    return jnp.dot(coords, second, preferred_element_type=jnp.float32)


KEY_BLOCK = 512


def attention_kernel(first_ref, bmin_ref, bmax_ref, qrange_ref, q_ref, k_ref, v_ref, qseg_ref,
                     kseg_ref, init_ref, o_ref, max_ref, sum_ref, acc_ref):
    j = pl.program_id(1)
    tok_rows = qseg_ref.shape[0]
    rows = q_ref.shape[1]
    group_size = rows // tok_rows
    first_pos = first_ref[0]
    low = jnp.maximum(first_pos - (WINDOW - 1), 0) // KEY_BLOCK
    high = (first_pos + tok_rows - 1) // KEY_BLOCK

    @pl.when(j == 0)
    def _():
        max_ref[...] = init_ref[0]
        sum_ref[...] = jnp.ones_like(sum_ref)
        acc_ref[...] = jnp.zeros_like(acc_ref)

    block = jnp.minimum(low + j, high)
    seg_low = bmin_ref[block]
    seg_high = bmax_ref[block]
    shares_segment = (seg_low == 0) | (
        (seg_high >= qrange_ref[0]) & (seg_low <= qrange_ref[1])
    )

    @pl.when((low + j <= high) & shares_segment)
    def _():
        scores = lax.dot_general(
            q_ref[0], k_ref[...], (((1,), (1,)), ((), ())),
            preferred_element_type=jnp.float32,
        ) * HD ** (-0.5)
        query_pos = first_pos + lax.broadcasted_iota(jnp.int32, (tok_rows, KEY_BLOCK), 0)
        key_pos = block * KEY_BLOCK + lax.broadcasted_iota(jnp.int32, (tok_rows, KEY_BLOCK), 1)
        key_seg = kseg_ref[...]
        allowed = (
            (key_pos <= query_pos)
            & (query_pos - key_pos < WINDOW)
            & ((key_seg == qseg_ref[...]) | (key_seg == 0))
        )
        scores = jnp.where(
            allowed[None], scores.reshape(group_size, tok_rows, KEY_BLOCK), NEGATIVE
        ).reshape(rows, KEY_BLOCK)
        prev_max = max_ref[...]
        new_max = jnp.maximum(prev_max, jnp.max(scores, axis=1, keepdims=True))
        factor = jnp.exp(prev_max - new_max)
        weights = jnp.exp(scores - new_max)
        sum_ref[...] = sum_ref[...] * factor + jnp.sum(weights, axis=1, keepdims=True)
        acc_ref[...] = acc_ref[...] * factor + jnp.dot(
            weights.astype(jnp.bfloat16), v_ref[...], preferred_element_type=jnp.float32
        )
        max_ref[...] = new_max

    @pl.when(j == pl.num_programs(1) - 1)
    def _():
        o_ref[0] = (acc_ref[...] / sum_ref[...]).astype(o_ref.dtype)


def window_attention(query_cols, key_piece, positions, segments, lengths, sink_logits):
    tok_rows = query_cols.shape[0]
    group_size = HEADS // KVH
    rows = group_size * tok_rows
    piece_rows = key_piece.shape[0]
    block_total = piece_rows // KEY_BLOCK
    steps = min(block_total, (WINDOW + tok_rows - 2) // KEY_BLOCK + 2)
    queries = jnp.transpose(
        query_cols.reshape(tok_rows, KVH, group_size, HD), (1, 2, 0, 3)
    ).reshape(KVH, rows, HD)
    key_seg = segment_of(jnp.arange(piece_rows, dtype=jnp.int32), lengths).reshape(1, piece_rows)
    query_seg = segments.reshape(tok_rows, 1)
    init = jnp.broadcast_to(
        sink_logits.reshape(KVH, group_size, 1, 1), (KVH, group_size, tok_rows, 1)
    ).reshape(KVH, rows, 1)
    first = positions[:1]
    block_seg = key_seg.reshape(block_total, KEY_BLOCK)
    block_min = jnp.min(block_seg, axis=1)
    block_max = jnp.max(block_seg, axis=1)
    query_range = jnp.stack([segments[0], segments[-1]])

    def key_block(h, j, first_ref, *_):
        f = first_ref[0]
        low = jnp.maximum(f - (WINDOW - 1), 0) // KEY_BLOCK
        high = (f + tok_rows - 1) // KEY_BLOCK
        return jnp.minimum(low + j, high)

    grid_spec = pltpu.PrefetchScalarGridSpec(
        num_scalar_prefetch=4,
        grid=(KVH, steps),
        in_specs=[
            pl.BlockSpec((1, rows, HD), lambda h, j, f, *_: (h, 0, 0)),
            pl.BlockSpec((KEY_BLOCK, HD), lambda h, j, f, *_: (key_block(h, j, f), h)),
            pl.BlockSpec((KEY_BLOCK, HD), lambda h, j, f, *_: (key_block(h, j, f), KVH + h)),
            pl.BlockSpec((tok_rows, 1), lambda h, j, f, *_: (0, 0)),
            pl.BlockSpec((1, KEY_BLOCK), lambda h, j, f, *_: (0, key_block(h, j, f))),
            pl.BlockSpec((1, rows, 1), lambda h, j, f, *_: (h, 0, 0)),
        ],
        out_specs=pl.BlockSpec((1, rows, HD), lambda h, j, f, *_: (h, 0, 0)),
        scratch_shapes=[
            pltpu.VMEM((rows, 1), jnp.float32),
            pltpu.VMEM((rows, 1), jnp.float32),
            pltpu.VMEM((rows, HD), jnp.float32),
        ],
    )
    out = pl.pallas_call(
        attention_kernel,
        grid_spec=grid_spec,
        out_shape=jax.ShapeDtypeStruct((KVH, rows, HD), jnp.bfloat16),
        compiler_params=pltpu.CompilerParams(dimension_semantics=("arbitrary", "arbitrary")),
    )(first, block_min, block_max, query_range, queries, key_piece, key_piece, query_seg, key_seg, init)
    return jnp.transpose(
        out.reshape(KVH, group_size, tok_rows, HD), (2, 0, 1, 3)
    ).reshape(tok_rows, HEADS * HD)


def gather_weights(attention_in, downs, ups, expert_up, axis_name):
    inner_width = attention_in.shape[0]
    in_width = attention_in.shape[1]
    down_cols = [jnp.transpose(f, (1, 0, 2)).reshape(inner_width, -1) for f in downs]
    local_adapters, local_experts, rank_size, hidden_width = expert_up.shape
    up_rows = [f.reshape(-1, f.shape[2]) for f in ups] + [
        jnp.transpose(expert_up, (0, 2, 1, 3)).reshape(local_adapters * rank_size, -1)
    ]
    wide = lax.all_gather(
        jnp.concatenate([attention_in] + down_cols, axis=1), axis_name, axis=1, tiled=True
    )
    peers = wide.shape[1] // (in_width + sum(c.shape[1] for c in down_cols))
    wide = wide.reshape(inner_width, peers, -1)
    full_in = wide[:, :, :in_width].reshape(inner_width, -1)
    joined = []
    offset = in_width
    for c in down_cols:
        joined.append(wide[:, :, offset : offset + c.shape[1]].reshape(inner_width, -1))
        offset += c.shape[1]
    tall = lax.all_gather(jnp.concatenate(up_rows, axis=1), axis_name, axis=0, tiled=True)
    seconds = []
    offset = 0
    for r in up_rows:
        seconds.append(tall[:, offset : offset + r.shape[1]])
        offset += r.shape[1]
    bank = jnp.transpose(
        seconds[-1].reshape(tall.shape[0], local_experts, hidden_width), (1, 0, 2)
    )
    return full_in, joined, seconds[:-1], bank


def body(
    tokens,
    segment_lengths,
    segment_adapters,
    routes,
    gate_weights,
    attention_gain,
    attention_in,
    sink_logits,
    attention_out,
    expert_gain,
    expert_gate_up,
    expert_down,
    adapter_in_down,
    adapter_in_up,
    adapter_out_down,
    adapter_out_up,
    adapter_expert_down,
    adapter_expert_up,
):
    tok_rows = tokens.shape[0]
    lengths = segment_lengths[0]
    segment_total = lengths.shape[0]
    first_pos = lax.axis_index("exp") * tok_rows
    positions = first_pos + jnp.arange(tok_rows, dtype=jnp.int32)
    segments = segment_of(positions, lengths)
    matches = segments[:, None] == jnp.arange(segment_total, dtype=jnp.int32)[None, :]
    token_adapter = jnp.sum(jnp.where(matches, segment_adapters[0][None, :], 0), axis=1)
    adapter_count = adapter_in_down.shape[0] * lax.axis_size("req")
    rank_size = adapter_in_down.shape[2]
    select = adapter_select(token_adapter, adapter_count, rank_size)
    normed = scaled_norm(tokens, attention_gain)
    full_in, joined, seconds, adapter_bank = gather_weights(
        attention_in,
        (adapter_in_down, adapter_out_down, adapter_expert_down),
        (adapter_in_up, adapter_out_up),
        adapter_expert_up,
        "req",
    )
    in_low, out_low, expert_low = joined
    in_high, out_high = seconds
    full_out = lax.all_gather(attention_out, "req", axis=1, tiled=True)
    base_heads = jnp.dot(normed, full_in, preferred_element_type=jnp.float32)
    projected = (base_heads + low_rank(normed, select, in_low, in_high)).astype(jnp.bfloat16)
    group_size = HEADS // KVH
    key_value = projected[:, HEADS * HD :]
    key_piece = lax.all_gather(key_value, "exp", axis=0, tiled=True)
    attended = window_attention(
        projected[:, : HEADS * HD], key_piece, positions, segments, lengths, sink_logits
    )
    base_out = jnp.dot(attended, full_out, preferred_element_type=jnp.float32)
    residual = (
        tokens.astype(jnp.float32) + base_out + low_rank(attended, select, out_low, out_high)
    ).astype(jnp.bfloat16)
    normed_two = scaled_norm(residual, expert_gain)
    low_parts = low_coords(normed_two, select, expert_low)
    top_count = routes.shape[1]
    picked = routes.reshape(-1)
    expert_hot = (picked[:, None] == jnp.arange(EXPERTS, dtype=jnp.int32)[None, :]).astype(
        jnp.int32
    )
    arrival = jnp.sum((jnp.cumsum(expert_hot, axis=0) - 1) * expert_hot, axis=1)
    slot_index = picked * CAP + arrival
    slot_count = EXPERTS * CAP
    slot_ids = jnp.arange(slot_count, dtype=jnp.int32)
    token_slots = slot_index.reshape(tok_rows, top_count)
    dispatch = jnp.any(
        token_slots[None, :, :] == slot_ids[:, None, None], axis=2
    ).astype(jnp.bfloat16)
    peer_count = lax.axis_size("exp")
    local_experts = EXPERTS // peer_count
    row_width = normed_two.shape[1]
    send = jnp.dot(
        dispatch,
        jnp.concatenate([normed_two, low_parts], axis=1),
        preferred_element_type=jnp.float32,
    ).astype(jnp.bfloat16).reshape(peer_count, local_experts, CAP, -1)
    hidden_width = expert_down.shape[1]

    def expert_chunk(chunk, gate_up_weights, bank, down_weights):
        arrived = lax.all_to_all(chunk, "exp", split_axis=0, concat_axis=0, tiled=True)
        arrived_rows = arrived[..., :row_width]
        arrived_low = arrived[..., row_width:]
        gate_up = jnp.einsum(
            "necd,edf->necf", arrived_rows, gate_up_weights, preferred_element_type=jnp.float32
        )
        up_part = gate_up[..., hidden_width:] + jnp.einsum(
            "necr,erf->necf", arrived_low, bank, preferred_element_type=jnp.float32
        )
        hidden = (jax.nn.relu(gate_up[..., :hidden_width]) * up_part).astype(jnp.bfloat16)
        outputs = jnp.einsum(
            "necf,efd->necd", hidden, down_weights, preferred_element_type=jnp.float32
        ).astype(jnp.bfloat16)
        return lax.all_to_all(outputs, "exp", split_axis=0, concat_axis=0, tiled=True)

    returned = jnp.concatenate(
        [
            expert_chunk(
                send[:, e : e + 1],
                expert_gate_up[e : e + 1],
                adapter_bank[e : e + 1],
                expert_down[e : e + 1],
            )
            for e in range(local_experts)
        ],
        axis=1,
    )
    flat_back = returned.reshape(EXPERTS * CAP, -1)
    gate_grid = jnp.sum(
        jnp.where(
            token_slots[:, :, None] == slot_ids[None, None, :], gate_weights[:, :, None], 0.0
        ),
        axis=1,
    )
    gate_high = gate_grid.astype(jnp.bfloat16)
    gate_low = (gate_grid - gate_high.astype(jnp.float32)).astype(jnp.bfloat16)
    combined = jnp.dot(gate_high, flat_back, preferred_element_type=jnp.float32) + jnp.dot(
        gate_low, flat_back, preferred_element_type=jnp.float32
    )
    return (residual.astype(jnp.float32) + combined).astype(jnp.bfloat16)


def solution(mesh):
    return jax.shard_map(
        body,
        mesh=mesh,
        in_specs=(
            P(("req", "exp"), None),
            P("req", None),
            P("req", None),
            P(("req", "exp"), None),
            P(("req", "exp"), None),
            P(),
            P(None, "req"),
            P(),
            P(None, "req"),
            P(),
            P("exp", None, None),
            P("exp", None, None),
            P("req", None, None),
            P("req", None, None),
            P("req", None, None),
            P("req", None, None),
            P("req", None, None),
            P("req", "exp", None, None),
        ),
        out_specs=P(("req", "exp"), None),
        check_vma=False,
    )
```

```python
import jax
import jax.numpy as jnp
from jax import lax
from jax.sharding import PartitionSpec as P
from jax.experimental import pallas as pl
from jax.experimental.pallas import tpu as pltpu

HEADS = 12
KVH = 2
HD = 128
EXPERTS = 32
WINDOW = 4096
CAP = 64


EPSILON = 1e-06
NEGATIVE = -1e30


def scaled_norm(inputs, gain):
    floats = inputs.astype(jnp.float32)
    inverse = lax.rsqrt(jnp.mean(floats * floats, axis=-1, keepdims=True) + EPSILON)
    return (floats * inverse * gain).astype(jnp.bfloat16)


def segment_of(positions, lengths):
    seg_ends = jnp.cumsum(lengths)
    return jnp.sum((positions[:, None] >= seg_ends[None, :]).astype(jnp.int32), axis=1)


def adapter_select(token_adapter, adapter_count, rank_size):
    owners = jnp.repeat(jnp.arange(adapter_count, dtype=jnp.int32), rank_size)
    return token_adapter[:, None] == owners[None, :]


def low_coords(inputs, select, joined):
    coords = jnp.dot(inputs, joined, preferred_element_type=jnp.float32)
    return jnp.where(select, coords, 0.0).astype(jnp.bfloat16)


def low_rank(inputs, select, joined, second):
    coords = low_coords(inputs, select, joined)
    return jnp.dot(coords, second, preferred_element_type=jnp.float32)


KEY_BLOCK = 1024


def attention_kernel(first_ref, bmin_ref, bmax_ref, qrange_ref, q_ref, k_ref, v_ref, qseg_ref,
                     kseg_ref, init_ref, o_ref, max_ref, sum_ref, acc_ref):
    j = pl.program_id(1)
    tok_rows = qseg_ref.shape[0]
    rows = q_ref.shape[1]
    group_size = rows // tok_rows
    first_pos = first_ref[0]
    low = jnp.maximum(first_pos - (WINDOW - 1), 0) // KEY_BLOCK
    high = (first_pos + tok_rows - 1) // KEY_BLOCK

    @pl.when(j == 0)
    def _():
        max_ref[...] = init_ref[0]
        sum_ref[...] = jnp.ones_like(sum_ref)
        acc_ref[...] = jnp.zeros_like(acc_ref)

    block = jnp.minimum(low + j, high)
    seg_low = bmin_ref[block]
    seg_high = bmax_ref[block]
    shares_segment = (seg_low == 0) | (
        (seg_high >= qrange_ref[0]) & (seg_low <= qrange_ref[1])
    )

    @pl.when((low + j <= high) & shares_segment)
    def _():
        scores = lax.dot_general(
            q_ref[0], k_ref[...], (((1,), (1,)), ((), ())),
            preferred_element_type=jnp.float32,
        ) * HD ** (-0.5)
        query_pos = first_pos + lax.broadcasted_iota(jnp.int32, (tok_rows, KEY_BLOCK), 0)
        key_pos = block * KEY_BLOCK + lax.broadcasted_iota(jnp.int32, (tok_rows, KEY_BLOCK), 1)
        key_seg = kseg_ref[...]
        allowed = (
            (key_pos <= query_pos)
            & (query_pos - key_pos < WINDOW)
            & ((key_seg == qseg_ref[...]) | (key_seg == 0))
        )
        scores = jnp.where(
            allowed[None], scores.reshape(group_size, tok_rows, KEY_BLOCK), NEGATIVE
        ).reshape(rows, KEY_BLOCK)
        prev_max = max_ref[...]
        new_max = jnp.maximum(prev_max, jnp.max(scores, axis=1, keepdims=True))
        factor = jnp.exp(prev_max - new_max)
        weights = jnp.exp(scores - new_max)
        sum_ref[...] = sum_ref[...] * factor + jnp.sum(weights, axis=1, keepdims=True)
        acc_ref[...] = acc_ref[...] * factor + jnp.dot(
            weights.astype(jnp.bfloat16), v_ref[...], preferred_element_type=jnp.float32
        )
        max_ref[...] = new_max

    @pl.when(j == pl.num_programs(1) - 1)
    def _():
        o_ref[0] = (acc_ref[...] / sum_ref[...]).astype(o_ref.dtype)


def window_attention(query_cols, key_piece, positions, segments, lengths, sink_logits):
    tok_rows = query_cols.shape[0]
    group_size = HEADS // KVH
    rows = group_size * tok_rows
    piece_rows = key_piece.shape[0]
    block_total = piece_rows // KEY_BLOCK
    steps = min(block_total, (WINDOW + tok_rows - 2) // KEY_BLOCK + 2)
    queries = jnp.transpose(
        query_cols.reshape(tok_rows, KVH, group_size, HD), (1, 2, 0, 3)
    ).reshape(KVH, rows, HD)
    key_seg = segment_of(jnp.arange(piece_rows, dtype=jnp.int32), lengths).reshape(1, piece_rows)
    query_seg = segments.reshape(tok_rows, 1)
    init = jnp.broadcast_to(
        sink_logits.reshape(KVH, group_size, 1, 1), (KVH, group_size, tok_rows, 1)
    ).reshape(KVH, rows, 1)
    first = positions[:1]
    block_seg = key_seg.reshape(block_total, KEY_BLOCK)
    block_min = jnp.min(block_seg, axis=1)
    block_max = jnp.max(block_seg, axis=1)
    query_range = jnp.stack([segments[0], segments[-1]])

    def key_block(h, j, first_ref, *_):
        f = first_ref[0]
        low = jnp.maximum(f - (WINDOW - 1), 0) // KEY_BLOCK
        high = (f + tok_rows - 1) // KEY_BLOCK
        return jnp.minimum(low + j, high)

    grid_spec = pltpu.PrefetchScalarGridSpec(
        num_scalar_prefetch=4,
        grid=(KVH, steps),
        in_specs=[
            pl.BlockSpec((1, rows, HD), lambda h, j, f, *_: (h, 0, 0)),
            pl.BlockSpec((KEY_BLOCK, HD), lambda h, j, f, *_: (key_block(h, j, f), h)),
            pl.BlockSpec((KEY_BLOCK, HD), lambda h, j, f, *_: (key_block(h, j, f), KVH + h)),
            pl.BlockSpec((tok_rows, 1), lambda h, j, f, *_: (0, 0)),
            pl.BlockSpec((1, KEY_BLOCK), lambda h, j, f, *_: (0, key_block(h, j, f))),
            pl.BlockSpec((1, rows, 1), lambda h, j, f, *_: (h, 0, 0)),
        ],
        out_specs=pl.BlockSpec((1, rows, HD), lambda h, j, f, *_: (h, 0, 0)),
        scratch_shapes=[
            pltpu.VMEM((rows, 1), jnp.float32),
            pltpu.VMEM((rows, 1), jnp.float32),
            pltpu.VMEM((rows, HD), jnp.float32),
        ],
    )
    out = pl.pallas_call(
        attention_kernel,
        grid_spec=grid_spec,
        out_shape=jax.ShapeDtypeStruct((KVH, rows, HD), jnp.bfloat16),
        compiler_params=pltpu.CompilerParams(dimension_semantics=("arbitrary", "arbitrary")),
    )(first, block_min, block_max, query_range, queries, key_piece, key_piece, query_seg, key_seg, init)
    return jnp.transpose(
        out.reshape(KVH, group_size, tok_rows, HD), (2, 0, 1, 3)
    ).reshape(tok_rows, HEADS * HD)


def gather_weights(attention_in, downs, ups, expert_up, axis_name):
    inner_width = attention_in.shape[0]
    in_width = attention_in.shape[1]
    down_cols = [jnp.transpose(f, (1, 0, 2)).reshape(inner_width, -1) for f in downs]
    local_adapters, local_experts, rank_size, hidden_width = expert_up.shape
    up_rows = [f.reshape(-1, f.shape[2]) for f in ups] + [
        jnp.transpose(expert_up, (0, 2, 1, 3)).reshape(local_adapters * rank_size, -1)
    ]
    wide = lax.all_gather(
        jnp.concatenate([attention_in] + down_cols, axis=1), axis_name, axis=1, tiled=True
    )
    peers = wide.shape[1] // (in_width + sum(c.shape[1] for c in down_cols))
    wide = wide.reshape(inner_width, peers, -1)
    full_in = wide[:, :, :in_width].reshape(inner_width, -1)
    joined = []
    offset = in_width
    for c in down_cols:
        joined.append(wide[:, :, offset : offset + c.shape[1]].reshape(inner_width, -1))
        offset += c.shape[1]
    tall = lax.all_gather(jnp.concatenate(up_rows, axis=1), axis_name, axis=0, tiled=True)
    seconds = []
    offset = 0
    for r in up_rows:
        seconds.append(tall[:, offset : offset + r.shape[1]])
        offset += r.shape[1]
    bank = jnp.transpose(
        seconds[-1].reshape(tall.shape[0], local_experts, hidden_width), (1, 0, 2)
    )
    return full_in, joined, seconds[:-1], bank


def body(
    tokens,
    segment_lengths,
    segment_adapters,
    routes,
    gate_weights,
    attention_gain,
    attention_in,
    sink_logits,
    attention_out,
    expert_gain,
    expert_gate_up,
    expert_down,
    adapter_in_down,
    adapter_in_up,
    adapter_out_down,
    adapter_out_up,
    adapter_expert_down,
    adapter_expert_up,
):
    tok_rows = tokens.shape[0]
    lengths = segment_lengths[0]
    segment_total = lengths.shape[0]
    first_pos = lax.axis_index("exp") * tok_rows
    positions = first_pos + jnp.arange(tok_rows, dtype=jnp.int32)
    segments = segment_of(positions, lengths)
    matches = segments[:, None] == jnp.arange(segment_total, dtype=jnp.int32)[None, :]
    token_adapter = jnp.sum(jnp.where(matches, segment_adapters[0][None, :], 0), axis=1)
    adapter_count = adapter_in_down.shape[0] * lax.axis_size("req")
    rank_size = adapter_in_down.shape[2]
    select = adapter_select(token_adapter, adapter_count, rank_size)
    normed = scaled_norm(tokens, attention_gain)
    full_in, joined, seconds, adapter_bank = gather_weights(
        attention_in,
        (adapter_in_down, adapter_out_down, adapter_expert_down),
        (adapter_in_up, adapter_out_up),
        adapter_expert_up,
        "req",
    )
    in_low, out_low, expert_low = joined
    in_high, out_high = seconds
    full_out = lax.all_gather(attention_out, "req", axis=1, tiled=True)
    base_heads = jnp.dot(normed, full_in, preferred_element_type=jnp.float32)
    projected = (base_heads + low_rank(normed, select, in_low, in_high)).astype(jnp.bfloat16)
    group_size = HEADS // KVH
    key_value = projected[:, HEADS * HD :]
    key_piece = lax.all_gather(key_value, "exp", axis=0, tiled=True)
    attended = window_attention(
        projected[:, : HEADS * HD], key_piece, positions, segments, lengths, sink_logits
    )
    base_out = jnp.dot(attended, full_out, preferred_element_type=jnp.float32)
    residual = (
        tokens.astype(jnp.float32) + base_out + low_rank(attended, select, out_low, out_high)
    ).astype(jnp.bfloat16)
    normed_two = scaled_norm(residual, expert_gain)
    low_parts = low_coords(normed_two, select, expert_low)
    top_count = routes.shape[1]
    picked = routes.reshape(-1)
    expert_hot = (picked[:, None] == jnp.arange(EXPERTS, dtype=jnp.int32)[None, :]).astype(
        jnp.int32
    )
    arrival = jnp.sum((jnp.cumsum(expert_hot, axis=0) - 1) * expert_hot, axis=1)
    slot_index = picked * CAP + arrival
    slot_count = EXPERTS * CAP
    slot_ids = jnp.arange(slot_count, dtype=jnp.int32)
    token_slots = slot_index.reshape(tok_rows, top_count)
    dispatch = jnp.any(
        token_slots[None, :, :] == slot_ids[:, None, None], axis=2
    ).astype(jnp.bfloat16)
    peer_count = lax.axis_size("exp")
    local_experts = EXPERTS // peer_count
    row_width = normed_two.shape[1]
    send = jnp.dot(
        dispatch,
        jnp.concatenate([normed_two, low_parts], axis=1),
        preferred_element_type=jnp.float32,
    ).astype(jnp.bfloat16).reshape(peer_count, local_experts, CAP, -1)
    hidden_width = expert_down.shape[1]

    def expert_chunk(chunk):
        arrived = lax.all_to_all(chunk, "exp", split_axis=0, concat_axis=0, tiled=True)
        arrived_rows = arrived[..., :row_width]
        arrived_low = arrived[..., row_width:]
        gate_up = jnp.einsum(
            "necd,edf->necf", arrived_rows, expert_gate_up, preferred_element_type=jnp.float32
        )
        up_part = gate_up[..., hidden_width:] + jnp.einsum(
            "necr,erf->necf", arrived_low, adapter_bank, preferred_element_type=jnp.float32
        )
        hidden = (jax.nn.relu(gate_up[..., :hidden_width]) * up_part).astype(jnp.bfloat16)
        outputs = jnp.einsum(
            "necf,efd->necd", hidden, expert_down, preferred_element_type=jnp.float32
        ).astype(jnp.bfloat16)
        return lax.all_to_all(outputs, "exp", split_axis=0, concat_axis=0, tiled=True)

    half = CAP // 2
    returned = jnp.concatenate(
        [expert_chunk(send[:, :, :half]), expert_chunk(send[:, :, half:])], axis=2
    )
    flat_back = returned.reshape(EXPERTS * CAP, -1)
    gate_grid = jnp.sum(
        jnp.where(
            token_slots[:, :, None] == slot_ids[None, None, :], gate_weights[:, :, None], 0.0
        ),
        axis=1,
    )
    gate_high = gate_grid.astype(jnp.bfloat16)
    gate_low = (gate_grid - gate_high.astype(jnp.float32)).astype(jnp.bfloat16)
    combined = jnp.dot(gate_high, flat_back, preferred_element_type=jnp.float32) + jnp.dot(
        gate_low, flat_back, preferred_element_type=jnp.float32
    )
    return (residual.astype(jnp.float32) + combined).astype(jnp.bfloat16)


def solution(mesh):
    return jax.shard_map(
        body,
        mesh=mesh,
        in_specs=(
            P(("req", "exp"), None),
            P("req", None),
            P("req", None),
            P(("req", "exp"), None),
            P(("req", "exp"), None),
            P(),
            P(None, "req"),
            P(),
            P(None, "req"),
            P(),
            P("exp", None, None),
            P("exp", None, None),
            P("req", None, None),
            P("req", None, None),
            P("req", None, None),
            P("req", None, None),
            P("req", None, None),
            P("req", "exp", None, None),
        ),
        out_specs=P(("req", "exp"), None),
        check_vma=False,
    )
```
